128 devices in a mesh: ctx: 8 (over y, z_hi), head: 4 (over z_lo, core), dp: 4 (over x).
Axes of the slice: x: 4, y: 4, z: 4 (z_hi: 2, z_lo: 2; z = z_hi * 2 + z_lo), core: 2. Of those that a mesh axis runs over, the one named last changes fastest.
Arguments:
- long_query: bfloat16 [24576, 8192], P(('dp', 'ctx', 'head')), parts along dimension 0, may hold values from -250 to 250
- long_kv: bfloat16 [2, 24576, 1024], P(None, ('dp', 'ctx', 'head')), parts along dimension 1, may hold values from -250 to 250
- short_query: bfloat16 [32768, 8192], P(('dp', 'ctx', 'head')), parts along dimension 0, may hold values from -250 to 250
- short_key_value: bfloat16 [2, 32768, 1024], P(None, ('dp', 'ctx', 'head')), parts along dimension 1, may hold values from -250 to 250
- short_seg: int32 [128, 256], P(('dp', 'ctx', 'head')), parts along dimension 0, may hold values from 0 to 7, never falling along the last dimension, each value on 1 to 128 neighbouring positions
Outputs:
- long_out: bfloat16 [24576, 8192], P(('dp', 'ctx', 'head')), parts along dimension 0
- short_out: bfloat16 [32768, 8192], P(('dp', 'ctx', 'head')), parts along dimension 0
The draws below stay inside these ranges and needn't reach their ends.
There are 4 independent parts, one for each index of `dp`. The reference program is written for one: setup_inputs(seed, part) draws one part's arguments, and reference() takes and returns one part's arrays. A program takes and returns all parts, laid end to end along the dimension named above; each array names one. Nothing has to cross between parts.
All inputs are finite; a program needn't handle non-finite values.
Results may differ from the reference program's by a relative error of at most 0.0035.
Values may be sent and summed in bfloat16 or wider, within the bound.
A program may use at most 256 MiB of HBM per device.

```python
import math
import jax
import jax.numpy as jnp
import numpy as np
from jax import lax

QUERY_HEAD_COUNT = 64
KEY_VALUE_HEADS = 8
HEAD_SIZE = 128
LONG_DEV = 192
SHORT_TOKENS = 256
WINDOW_DEVICES = 32
LONG = 6144
SHORT = 8192


def make_fields(key, count_of_rows, block_extent):
    piece_list = jax.random.split(key, 4)
    query_rows = jnp.clip(jax.random.normal(piece_list[0], (count_of_rows, QUERY_HEAD_COUNT, HEAD_SIZE), jnp.float32), -4.0, 4.0)
    key_collection = jnp.clip(jax.random.normal(piece_list[1], (count_of_rows, KEY_VALUE_HEADS, HEAD_SIZE), jnp.float32), -4.0, 4.0)
    random_shift = 0.5 * jax.random.normal(piece_list[2], (count_of_rows, KEY_VALUE_HEADS * HEAD_SIZE), jnp.float32)
    center_points = jax.random.normal(piece_list[3], (count_of_rows // block_extent, KEY_VALUE_HEADS * HEAD_SIZE), jnp.float32)
    value_rows = random_shift + jnp.repeat(center_points, block_extent, axis=0)
    query_out = query_rows.reshape(count_of_rows, QUERY_HEAD_COUNT * HEAD_SIZE).astype(jnp.bfloat16)
    stacked_rows = jnp.stack([key_collection.reshape(count_of_rows, KEY_VALUE_HEADS * HEAD_SIZE), value_rows]).astype(jnp.bfloat16)
    return (query_out, stacked_rows)


def draw_long_query(key, part):
    return make_fields(jax.random.fold_in(key, 11), LONG, LONG_DEV)[0]


def draw_long_kv(key, part):
    return make_fields(jax.random.fold_in(key, 11), LONG, LONG_DEV)[1]


def draw_short_query(key, part):
    return make_fields(jax.random.fold_in(key, 23), SHORT, SHORT_TOKENS // 4)[0]


def draw_short_key_value(key, part):
    return make_fields(jax.random.fold_in(key, 23), SHORT, SHORT_TOKENS // 4)[1]


def length_profile(number_of, total, limit, skew):
    loads = [(1 << 20) // math.isqrt(standing ** skew) + 1 for standing in range(2, number_of + 1)]
    rest, holding = total - limit - (number_of - 1), [1] * (number_of - 1)
    while rest > 0:
        candidates = [i for i in range(number_of - 1) if holding[i] < limit]
        whole, left = sum([loads[i] for i in candidates]), rest
        for i in candidates:
            addition = min(limit - holding[i], max(1, left * loads[i] // whole), rest)
            holding[i] = holding[i] + addition
            rest = rest - addition
    return np.array([limit] + holding)


def ragged(own_key, count, total, bound, lean):
    if count == 2:
        one = jax.random.randint(own_key, (), max(1, total - bound), min(bound, total - 1) + 1)
        return jnp.stack([one, total - one])
    sizes = jnp.asarray(length_profile(count, total, bound, lean), jnp.int32)
    twos = (count - 1) // 2
    giver, sink = sizes[1:1 + 2 * twos:2], sizes[2:2 + 2 * twos:2]
    slack = jnp.minimum(giver - 1, bound - sink)
    moved = jax.random.randint(jax.random.fold_in(own_key, 1), (twos,), 0, 1 << 20) % (slack + 1)
    sizes = sizes.at[1:1 + 2 * twos:2].set(giver - moved).at[2:2 + 2 * twos:2].set(sink + moved)
    return sizes[jax.random.permutation(jax.random.fold_in(own_key, 2), count)]


def setup_inputs(seed: int = 0, part: int = 0) -> dict:
    streams_of = jax.random.split(jax.random.key(seed), 6)
    own_keys = jax.random.split(jax.random.fold_in(streams_of[5], part), 6)
    long_query = draw_long_query(jax.random.fold_in(jax.random.fold_in(streams_of[5], part), 71), part)
    long_kv = draw_long_kv(jax.random.fold_in(jax.random.fold_in(streams_of[5], part), 71), part)
    short_query = draw_short_query(jax.random.fold_in(jax.random.fold_in(streams_of[5], part), 71), part)
    short_key_value = draw_short_key_value(jax.random.fold_in(jax.random.fold_in(streams_of[5], part), 71), part)
    short_seg = jax.vmap(lambda own: jnp.searchsorted(jnp.cumsum(ragged(own, 8, SHORT_TOKENS, SHORT_TOKENS // 2, 2)), jnp.arange(SHORT_TOKENS), side="right"))(jax.random.split(own_keys[4], WINDOW_DEVICES)).reshape((WINDOW_DEVICES, SHORT_TOKENS)).astype(jnp.int32)
    return {"long_query": long_query, "long_kv": long_kv, "short_query": short_query, "short_key_value": short_key_value, "short_seg": short_seg}


def attend_rows(query_rows, stacked_rows, positions, labels):
    count_of_rows = query_rows.shape[0]
    query_heads = query_rows.reshape(count_of_rows, QUERY_HEAD_COUNT, HEAD_SIZE).transpose(1, 0, 2)
    key_head_rows = stacked_rows[0].reshape(count_of_rows, KEY_VALUE_HEADS, HEAD_SIZE).transpose(1, 0, 2)
    value_head_rows = stacked_rows[1].reshape(count_of_rows, KEY_VALUE_HEADS, HEAD_SIZE).transpose(1, 0, 2)
    allowed = (positions[None, :] <= positions[:, None]) & (labels[None, :] == labels[:, None])

    def one_head(head_number):
        group_number = head_number // (QUERY_HEAD_COUNT // KEY_VALUE_HEADS)
        scores = jnp.dot(query_heads[head_number], key_head_rows[group_number].T, preferred_element_type=jnp.float32) * (1.0 / math.sqrt(HEAD_SIZE))
        masked = jnp.where(allowed, scores, -1e+30)
        highest = lax.optimization_barrier(jnp.max(masked, axis=-1, keepdims=True))
        weights = jnp.where(allowed, jnp.exp(scores - highest), 0.0)
        totals = lax.optimization_barrier(jnp.sum(weights, axis=-1, keepdims=True))
        mixed = jnp.dot(weights.astype(jnp.bfloat16), value_head_rows[group_number], preferred_element_type=jnp.float32) / totals
        return mixed.astype(jnp.bfloat16)
    heads_out = lax.map(one_head, jnp.arange(QUERY_HEAD_COUNT, dtype=jnp.int32))
    return heads_out.transpose(1, 0, 2).reshape(count_of_rows, QUERY_HEAD_COUNT * HEAD_SIZE)

def attend_device(bundle):
    positions = jnp.arange(SHORT_TOKENS, dtype=jnp.int32)
    return attend_rows(bundle[0], bundle[1], positions, bundle[2])

def reference(long_query, long_kv, short_query, short_key_value, short_seg):
    positions = jnp.arange(LONG, dtype=jnp.int32)
    labels = jnp.zeros((LONG,), jnp.int32)
    long_out = attend_rows(long_query, long_kv, positions, labels)
    device_q = short_query.reshape(WINDOW_DEVICES, SHORT_TOKENS, QUERY_HEAD_COUNT * HEAD_SIZE)
    device_key_value = short_key_value.reshape(2, WINDOW_DEVICES, SHORT_TOKENS, KEY_VALUE_HEADS * HEAD_SIZE).transpose(1, 0, 2, 3)
    short_out = lax.map(attend_device, (device_q, device_key_value, short_seg)).reshape(SHORT, QUERY_HEAD_COUNT * HEAD_SIZE)
    return (long_out, short_out)
```

```python
import functools
import math

import jax
import jax.numpy as jnp
from jax import lax
from jax.experimental import pallas as pl
from jax.experimental.pallas import tpu as pltpu
from jax.sharding import PartitionSpec as P

QUERY_HEAD_COUNT = 64
KEY_VALUE_HEADS = 8
HEAD_SIZE = 128
GROUP = QUERY_HEAD_COUNT // KEY_VALUE_HEADS

NEG_LARGE = -1e30
LOG2_SCALE = math.log2(math.e) / math.sqrt(HEAD_SIZE)
PIECE_HEADS = 2
KEY_BLOCK = 1536


def dot_nt(a, b):
    return lax.dot_general(a, b, (((1,), (1,)), ((), ())), preferred_element_type=jnp.float32)


def long_kernel(q_ref, k_ref, v_ref, held_ref, o_ref, acc, high, total, *, rows, block):
    shards, tokens = k_ref.shape[0], k_ref.shape[1]
    per_block = block // tokens
    rank = lax.axis_index("ctx") * lax.axis_size("head") + lax.axis_index("head")
    full = rank // per_block
    acc[...] = jnp.zeros_like(acc)
    total[...] = jnp.zeros_like(total)
    high[...] = jnp.full_like(high, NEG_LARGE)

    def one_block(index, masked):
        shard = pl.multiple_of(index * per_block, per_block)
        k = k_ref[pl.ds(shard, per_block)].reshape(block, HEAD_SIZE)
        v = v_ref[pl.ds(shard, per_block)].reshape(block, HEAD_SIZE)
        v_one = jnp.concatenate([v, jnp.ones_like(v)], axis=1)
        if masked:
            q_pos = (rank - shard) * tokens + lax.broadcasted_iota(jnp.int32, (rows, block), 0)
            allowed = lax.broadcasted_iota(jnp.int32, (rows, block), 1) <= q_pos
        for h in range(GROUP):
            r = slice(h * rows, (h + 1) * rows)
            s = dot_nt(q_ref[:, h * HEAD_SIZE : (h + 1) * HEAD_SIZE], k)
            if masked:
                s = jnp.where(allowed, s, NEG_LARGE)
            old = high[r, :]
            new = jnp.maximum(old, jnp.max(s, axis=1, keepdims=True) * LOG2_SCALE)
            factor = jnp.exp2(old - new)
            p = jnp.exp2(s * LOG2_SCALE - new[:, :1]).astype(jnp.bfloat16)
            mixed = jnp.dot(p, v_one, preferred_element_type=jnp.float32)
            high[r, :] = new
            acc[r, :] = acc[r, :] * factor + mixed[:, :HEAD_SIZE]
            total[r, :] = total[r, :] * factor + mixed[:, HEAD_SIZE:]

    def body(index, carry):
        one_block(index, False)
        return carry

    lax.fori_loop(0, full, body, 0)
    one_block(full, True)
    for h in range(GROUP):
        r = slice(h * rows, (h + 1) * rows)
        o_ref[:, h * HEAD_SIZE : (h + 1) * HEAD_SIZE] = (acc[r, :] / total[r, :]).astype(o_ref.dtype)


def long_piece(query, gathered, held, piece):
    rows = query.shape[0]
    shards, _, tokens, width = gathered.shape
    heads = width // HEAD_SIZE
    first = piece * heads
    wide = GROUP * HEAD_SIZE
    flops = heads * GROUP * rows * shards * tokens * HEAD_SIZE * 4
    args = [query, gathered, gathered]
    in_specs = [
        pl.BlockSpec((rows, wide), lambda g: (0, first + g)),
        pl.BlockSpec((shards, None, tokens, HEAD_SIZE), lambda g: (0, 0, 0, g)),
        pl.BlockSpec((shards, None, tokens, HEAD_SIZE), lambda g: (0, 1, 0, g)),
    ]
    kernel = functools.partial(long_kernel, rows=rows, block=KEY_BLOCK)
    aliases = {}
    if held is None:
        body = lambda q, k, v, o, *rest: kernel(q, k, v, None, o, *rest)
    else:
        body = kernel
        args.append(held)
        in_specs.append(pl.BlockSpec(memory_space=pl.ANY))
        aliases = {3: 0}
    return pl.pallas_call(
        body,
        out_shape=jax.ShapeDtypeStruct(query.shape, query.dtype),
        grid=(heads,),
        in_specs=in_specs,
        out_specs=pl.BlockSpec((rows, wide), lambda g: (0, first + g)),
        scratch_shapes=[pltpu.VMEM((GROUP * rows, HEAD_SIZE), jnp.float32)] * 3,
        input_output_aliases=aliases,
        compiler_params=pltpu.CompilerParams(vmem_limit_bytes=50 << 20),
        cost_estimate=pl.CostEstimate(flops=flops, bytes_accessed=8 << 20, transcendentals=flops // 512),
        name=f"long_piece_{piece}",
    )(*args)


def short_kernel(q_ref, k_ref, v_ref, seg_row_ref, seg_col_ref, o_ref):
    tokens = q_ref.shape[0]
    half = tokens // 2
    k, v = k_ref[...], v_ref[...]
    v_one = jnp.concatenate([v, jnp.ones_like(v)], axis=1)
    labels_q = seg_col_ref[...]
    labels_k = seg_row_ref[...]
    for part in range(2):
        low, keys = part * half, (part + 1) * half
        q_pos = low + lax.broadcasted_iota(jnp.int32, (half, keys), 0)
        k_pos = lax.broadcasted_iota(jnp.int32, (half, keys), 1)
        same = labels_q[low : low + half, :1] == labels_k[:1, :keys]
        allowed = (k_pos <= q_pos) & same
        for h in range(GROUP):
            c = slice(h * HEAD_SIZE, (h + 1) * HEAD_SIZE)
            s = dot_nt(q_ref[low : low + half, c], k[:keys])
            s = jnp.where(allowed, s, NEG_LARGE)
            top = jnp.max(s, axis=1, keepdims=True)
            p = jnp.exp2((s - top) * LOG2_SCALE).astype(jnp.bfloat16)
            mixed = jnp.dot(p, v_one[:keys], preferred_element_type=jnp.float32)
            o_ref[low : low + half, c] = (mixed[:, :HEAD_SIZE] / mixed[:, HEAD_SIZE:]).astype(o_ref.dtype)


def attend_short(query, key_value, seg):
    tokens = query.shape[0]
    wide = GROUP * HEAD_SIZE
    seg_row = jnp.broadcast_to(seg, (8, tokens))
    seg_col = jnp.broadcast_to(seg.reshape(tokens, 1), (tokens, HEAD_SIZE))
    flops = QUERY_HEAD_COUNT * tokens * tokens * HEAD_SIZE * 4
    return pl.pallas_call(
        short_kernel,
        out_shape=jax.ShapeDtypeStruct(query.shape, query.dtype),
        grid=(KEY_VALUE_HEADS,),
        in_specs=[
            pl.BlockSpec((tokens, wide), lambda g: (0, g)),
            pl.BlockSpec((None, tokens, HEAD_SIZE), lambda g: (0, 0, g)),
            pl.BlockSpec((None, tokens, HEAD_SIZE), lambda g: (1, 0, g)),
            pl.BlockSpec((8, tokens), lambda g: (0, 0)),
            pl.BlockSpec((tokens, HEAD_SIZE), lambda g: (0, 0)),
        ],
        out_specs=pl.BlockSpec((tokens, wide), lambda g: (0, g)),
        cost_estimate=pl.CostEstimate(flops=flops, bytes_accessed=9 << 20, transcendentals=flops // 512),
        name="short_docs",
    )(query, key_value, key_value, seg_row, seg_col)


def on_device(long_query, long_kv, short_query, short_key_value, short_seg):
    width = PIECE_HEADS * HEAD_SIZE
    gathered = []
    for piece in range(KEY_VALUE_HEADS // PIECE_HEADS):
        part = long_kv[:, :, piece * width : (piece + 1) * width]
        gathered.append(lax.all_gather(part, ("ctx", "head"), axis=0, tiled=False))
    short_out = attend_short(short_query, short_key_value, short_seg)
    long_out = None
    for piece, part in enumerate(gathered):
        long_out = long_piece(long_query, part, long_out, piece)
    return (long_out, short_out)


def solution(mesh):
    return jax.shard_map(
        on_device,
        mesh=mesh,
        in_specs=(
            P(("dp", "ctx", "head"), None),
            P(None, ("dp", "ctx", "head"), None),
            P(("dp", "ctx", "head"), None),
            P(None, ("dp", "ctx", "head"), None),
            P(("dp", "ctx", "head"), None),
        ),
        out_specs=(P(("dp", "ctx", "head"), None), P(("dp", "ctx", "head"), None)),
        check_vma=False,
    )
```

```python
import functools
import math

import jax
import jax.numpy as jnp
from jax import lax
from jax.experimental import pallas as pl
from jax.experimental.pallas import tpu as pltpu
from jax.sharding import PartitionSpec as P

QUERY_HEAD_COUNT = 64
KEY_VALUE_HEADS = 8
HEAD_SIZE = 128
GROUP = QUERY_HEAD_COUNT // KEY_VALUE_HEADS
WIDE = GROUP * HEAD_SIZE

NEG_LARGE = -1e30
LOG2_SCALE = math.log2(math.e) / math.sqrt(HEAD_SIZE)

SIDE = 4
LOCAL_HEADS = KEY_VALUE_HEADS // 2
PAIR = LOCAL_HEADS // 2
PAIR_WIDTH = PAIR * HEAD_SIZE
MESH = pl.DeviceIdType.MESH

NEAR, FAR, RESULT, COPIES = 3, 11, 43, 45


def dot_nt(a, b):
    return lax.dot_general(a, b, (((1,), (1,)), ((), ())), preferred_element_type=jnp.float32)


def wrap(x):
    return lax.rem(x + SIDE, SIDE)


def order_of(index, half, core):
    return jnp.where(index < half, core * half + index, (1 - core) * half + index - half)


def kernel(
    q_hbm, kv_hbm, short_q_hbm, short_kv_hbm, seg_row, seg_col, out_hbm, short_out_hbm,
    q, kv, acc, high, total, score_0, score_1, result, short_q, short_kv, send, recv, local,
):
    half = q_hbm.shape[0]
    rows = 2 * half
    ctx, head = lax.axis_index("ctx"), lax.axis_index("head")
    y, z, core = lax.div(ctx, 2), lax.rem(ctx, 2) * 2 + lax.div(head, 2), lax.rem(head, 2)
    chip = y * SIDE + z
    q_columns = LOCAL_HEADS * WIDE

    def device(to_y, to_z, to_core):
        return {"ctx": to_y * 2 + lax.div(to_z, 2), "head": lax.rem(to_z, 2) * 2 + to_core}

    mate = device(y, z, 1 - core)
    ahead = (device(y, wrap(z + 1), core), device(wrap(y + 1), z, core))
    behind = (device(y, wrap(z - 1), core), device(wrap(y - 1), z, core))

    def remote(src, dst, index, target):
        return pltpu.make_async_remote_copy(
            src_ref=src, dst_ref=dst, send_sem=send.at[index], recv_sem=recv.at[index], device_id=target, device_id_type=MESH
        )

    def mine_columns(side, of_core):
        start = of_core * (LOCAL_HEADS * HEAD_SIZE) + side * PAIR_WIDTH
        return pl.ds(pl.multiple_of(start, PAIR_WIDTH), PAIR_WIDTH)

    def heads_of(of_core, start, size):
        return pl.ds(pl.multiple_of(of_core * q_columns + start, size), size)

    def mate_kv(side):
        return remote(kv_hbm.at[:, :, mine_columns(side, 1 - core)], kv.at[side, 0, :, 0, pl.ds(half, half)], 1 + side, mate)

    def mate_q():
        return remote(q_hbm.at[:, heads_of(1 - core, 0, q_columns)], q.at[1], 0, mate)

    def near(side, which):
        index = NEAR + 4 * side + which
        if which == 0:
            return remote(kv.at[side, 0, :, 0], kv.at[side, 0, :, 1], index, ahead[side])
        if which == 1:
            return remote(kv.at[side, 0, :, 0], kv.at[side, 0, :, 2], index, behind[side])
        if which == 2:
            return remote(kv.at[side, 0, 0, 1], kv.at[side, 0, 0, 3], index, ahead[side])
        return remote(kv.at[side, 0, 1, 2], kv.at[side, 0, 1, 3], index, behind[side])

    def far(side, piece, which):
        index = FAR + 16 * side + 4 * piece + which
        unit, slot = 1 + piece // 2, 2 * (piece % 2)
        if which == 0:
            return remote(kv.at[side, 0, :, piece], kv.at[side, unit, :, slot], index, ahead[1 - side])
        if which == 1:
            return remote(kv.at[side, 0, :, piece], kv.at[side, unit, :, slot + 1], index, behind[1 - side])
        if which == 2:
            return remote(kv.at[side, unit, 0, slot], kv.at[side, 3, 0, piece], index, ahead[1 - side])
        return remote(kv.at[side, unit, 1, slot + 1], kv.at[side, 3, 1, piece], index, behind[1 - side])

    def give_back(side):
        columns = heads_of(core, side * (PAIR * WIDE), PAIR * WIDE)
        return remote(result.at[1, side], out_hbm.at[:, columns], RESULT + side, mate)

    def keep(side):
        columns = heads_of(core, side * (PAIR * WIDE), PAIR * WIDE)
        return pltpu.make_async_copy(result.at[0, side], out_hbm.at[:, columns], local.at[5 + side])

    own_q = pltpu.make_async_copy(q_hbm.at[:, heads_of(core, 0, q_columns)], q.at[0], local.at[0])
    own_kv = [
        pltpu.make_async_copy(kv_hbm.at[:, :, mine_columns(side, core)], kv.at[side, 0, :, 0, pl.ds(0, half)], local.at[1 + side])
        for side in range(2)
    ]
    get_short_q = pltpu.make_async_copy(short_q_hbm, short_q, local.at[3])
    get_short_kv = pltpu.make_async_copy(short_kv_hbm, short_kv, local.at[4])
    put_short = pltpu.make_async_copy(short_q, short_out_hbm, local.at[7])

    own_kv[0].start()
    own_kv[1].start()
    barrier = pltpu.get_barrier_semaphore()
    for target in (mate,) + ahead + behind:
        pl.semaphore_signal(barrier, inc=1, device_id=target, device_id_type=MESH)
    pl.semaphore_wait(barrier, 5)
    for side in range(2):
        mate_kv(side).start()
    mate_q().start()
    get_short_kv.start()
    get_short_q.start()
    own_q.start()
    for side in range(2):
        own_kv[side].wait()
        mate_kv(side).wait_recv()
        near(side, 0).start()
        near(side, 1).start()
    for side in range(2):
        far(side, 0, 0).start()
        far(side, 0, 1).start()

    tokens = short_q.shape[0]
    part_rows = tokens // 2

    def short_head(g, carry):
        key_columns = pl.ds(pl.multiple_of(g * HEAD_SIZE, HEAD_SIZE), HEAD_SIZE)
        k, v = short_kv[0, :, key_columns], short_kv[1, :, key_columns]
        v_one = jnp.concatenate([v, jnp.ones_like(v)], axis=1)
        columns = [pl.ds(pl.multiple_of(g * WIDE + h * HEAD_SIZE, HEAD_SIZE), HEAD_SIZE) for h in range(GROUP)]
        for part in range(2):
            low, keys = part * part_rows, (part + 1) * part_rows
            q_pos = low + lax.broadcasted_iota(jnp.int32, (part_rows, keys), 0)
            k_pos = lax.broadcasted_iota(jnp.int32, (part_rows, keys), 1)
            same = seg_col[low : low + part_rows, :1] == seg_row[:1, :keys]
            allowed = (k_pos <= q_pos) & same
            weights = []
            for s in [dot_nt(short_q[low : low + part_rows, c], k[:keys]) for c in columns]:
                s = jnp.where(allowed, s, NEG_LARGE)
                top = jnp.max(s, axis=1, keepdims=True)
                weights.append(jnp.exp2((s - top) * LOG2_SCALE).astype(jnp.bfloat16))
            mixes = [jnp.dot(p, v_one[:keys], preferred_element_type=jnp.float32) for p in weights]
            for c, mixed in zip(columns, mixes):
                short_q[low : low + part_rows, c] = (mixed[:, :HEAD_SIZE] / mixed[:, HEAD_SIZE:]).astype(jnp.bfloat16)
        return carry

    get_short_kv.wait()
    get_short_q.wait()

    def short_step(g, carry):
        short_head(g, carry)

        @pl.when(g == 5)
        def _():
            for side in range(2):
                near(side, 0).wait_recv()
                near(side, 2).start()
                near(side, 1).wait_recv()
                near(side, 3).start()
            for piece in (1, 2):
                for side in range(2):
                    far(side, piece, 0).start()
                    far(side, piece, 1).start()

        return carry

    lax.fori_loop(0, KEY_VALUE_HEADS, short_step, 0)
    put_short.start()
    own_q.wait()
    mate_q().wait_recv()
    for side in range(2):
        near(side, 2).wait_recv()
        near(side, 3).wait_recv()
        far(side, 3, 0).start()
        far(side, 3, 1).start()

    q_pos = chip * rows + order_of(lax.broadcasted_iota(jnp.int32, (rows, 1), 0), half, core)
    key_index = order_of(lax.broadcasted_iota(jnp.int32, (1, rows), 1), half, core)

    def phase(number, carry):
        unit, side = lax.div(number, 2), lax.rem(number, 2)
        owners = []
        for slot in range(SIDE):
            beyond = lax.div(slot, 2) + 2 * (unit - 1)
            ring = jnp.where(jnp.logical_or(unit == 0, unit == 3), slot, beyond)
            along = jnp.where(ring == 1, -1, jnp.where(ring == 2, 1, jnp.where(ring == 3, 2, 0)))
            across = jnp.where(unit == 0, 0, jnp.where(unit == 3, 2, 2 * (slot % 2) - 1))
            owner_y = wrap(y + jnp.where(side == 0, across, along))
            owner_z = wrap(z + jnp.where(side == 0, along, across))
            owners.append(owner_y * SIDE + owner_z)
        low = jnp.minimum(jnp.minimum(owners[0], owners[1]), jnp.minimum(owners[2], owners[3]))
        top = jnp.maximum(jnp.maximum(owners[0], owners[1]), jnp.maximum(owners[2], owners[3]))

        def block(local_head, plane):
            columns = pl.ds(pl.multiple_of(local_head * HEAD_SIZE, HEAD_SIZE), HEAD_SIZE)
            return kv[side, unit, plane, :, :, columns].reshape(SIDE * rows, HEAD_SIZE)

        def scores(item):
            columns = pl.ds(pl.multiple_of((side * PAIR * GROUP + item) * HEAD_SIZE, HEAD_SIZE), HEAD_SIZE)
            query = jnp.concatenate([q[0, :, columns], q[1, :, columns]], axis=0)
            return dot_nt(query, block(lax.div(item, GROUP), 0))

        def update(item, score, masked, first):
            v = block(lax.div(item, GROUP), 1)
            v_one = jnp.concatenate([v, jnp.ones_like(v)], axis=1)
            s = score[...]
            if masked:
                k_pos = jnp.concatenate([owner * rows + key_index for owner in owners], axis=1)
                s = jnp.where(k_pos <= q_pos, s, NEG_LARGE)
            r = pl.ds(pl.multiple_of((side * PAIR * GROUP + item) * rows, rows), rows)
            best = jnp.max(s, axis=1, keepdims=True) * LOG2_SCALE
            if first:
                new = jnp.broadcast_to(best, (rows, HEAD_SIZE))
            else:
                old = high[r, :]
                new = jnp.maximum(old, best)
                factor = jnp.exp2(old - new)
            p = jnp.exp2(s * LOG2_SCALE - new[:, :1]).astype(jnp.bfloat16)
            mixed = jnp.dot(p, v_one, preferred_element_type=jnp.float32)
            high[r, :] = new
            if first:
                acc[r, :] = mixed[:, :HEAD_SIZE]
                total[r, :] = mixed[:, HEAD_SIZE:]
            else:
                acc[r, :] = acc[r, :] * factor + mixed[:, :HEAD_SIZE]
                total[r, :] = total[r, :] * factor + mixed[:, HEAD_SIZE:]

        def run(masked, first):
            items = PAIR * GROUP
            score_0[...] = scores(0)

            def two(couple, inner):
                item = couple * 2
                score_1[...] = scores(item + 1)
                update(item, score_0, masked, first)
                score_0[...] = scores(jnp.minimum(item + 2, items - 1))
                update(item + 1, score_1, masked, first)
                return inner

            lax.fori_loop(0, items // 2, two, 0)

        @pl.when(unit == 0)
        def _():
            run(True, True)

        used = jnp.logical_and(unit > 0, low <= chip)

        @pl.when(jnp.logical_and(used, top < chip))
        def _():
            run(False, False)

        @pl.when(jnp.logical_and(used, top >= chip))
        def _():
            run(True, False)

        def pass_on(pieces):
            for piece in pieces:
                for side in range(2):
                    far(side, piece, 0).wait_recv()
                    far(side, piece, 2).start()
                    far(side, piece, 1).wait_recv()
                    far(side, piece, 3).start()

        @pl.when(number == 0)
        def _():
            pass_on((0,))

        @pl.when(number == 1)
        def _():
            pass_on((1,))

        @pl.when(number == 3)
        def _():
            pass_on((2, 3))

        @pl.when(number == 5)
        def _():
            for piece in range(SIDE):
                for side in range(2):
                    far(side, piece, 2).wait_recv()
                    far(side, piece, 3).wait_recv()

        @pl.when(unit == 3)
        def _():
            def divide(item, inner):
                r = pl.multiple_of((side * PAIR * GROUP + item) * rows, rows)
                columns = pl.ds(pl.multiple_of(item * HEAD_SIZE, HEAD_SIZE), HEAD_SIZE)
                for who in range(2):
                    part = pl.ds(r + who * half, half)
                    result[who, side, :, columns] = (acc[part, :] / total[part, :]).astype(jnp.bfloat16)
                return inner

            lax.fori_loop(0, PAIR * GROUP, divide, 0)

        for of_side in range(2):

            @pl.when(number == 6 + of_side)
            def _(of_side=of_side):
                give_back(of_side).start()
                keep(of_side).start()

        return carry

    lax.fori_loop(0, 8, phase, 0)

    put_short.wait()
    for side in range(2):
        keep(side).wait()
        give_back(side).wait_recv()
        give_back(side).wait_send()
        mate_kv(side).wait_send()
        for which in range(4):
            near(side, which).wait_send()
            for piece in range(SIDE):
                far(side, piece, which).wait_send()
    mate_q().wait_send()


def on_device(long_query, long_kv, short_query, short_key_value, short_seg):
    half, tokens = long_query.shape[0], short_query.shape[0]
    rows = 2 * half
    state_rows = LOCAL_HEADS * GROUP * rows
    seg_row = jnp.broadcast_to(short_seg, (8, tokens))
    seg_col = jnp.broadcast_to(short_seg.reshape(tokens, 1), (tokens, HEAD_SIZE))
    anywhere = pl.BlockSpec(memory_space=pl.ANY)
    vmem = pl.BlockSpec(memory_space=pltpu.VMEM)
    return pl.pallas_call(
        kernel,
        out_shape=(
            jax.ShapeDtypeStruct(long_query.shape, long_query.dtype),
            jax.ShapeDtypeStruct(short_query.shape, short_query.dtype),
        ),
        in_specs=[anywhere] * 4 + [vmem] * 2,
        out_specs=(anywhere, anywhere),
        scratch_shapes=[
            pltpu.VMEM((2, half, LOCAL_HEADS * WIDE), jnp.bfloat16),
            pltpu.VMEM((2, 4, 2, SIDE, rows, PAIR_WIDTH), jnp.bfloat16),
            pltpu.VMEM((state_rows, HEAD_SIZE), jnp.float32),
            pltpu.VMEM((state_rows, HEAD_SIZE), jnp.float32),
            pltpu.VMEM((state_rows, HEAD_SIZE), jnp.float32),
            pltpu.VMEM((rows, SIDE * rows), jnp.float32),
            pltpu.VMEM((rows, SIDE * rows), jnp.float32),
            pltpu.VMEM((2, 2, half, PAIR * WIDE), jnp.bfloat16),
            pltpu.VMEM(short_query.shape, jnp.bfloat16),
            pltpu.VMEM(short_key_value.shape, jnp.bfloat16),
            pltpu.SemaphoreType.DMA((COPIES,)),
            pltpu.SemaphoreType.DMA((COPIES,)),
            pltpu.SemaphoreType.DMA((8,)),
        ],
        compiler_params=pltpu.CompilerParams(
            collective_id=0, has_side_effects=True, vmem_limit_bytes=63 << 20
        ),
        name="window_attention",
    )(long_query, long_kv, short_query, short_key_value, seg_row, seg_col)


def solution(mesh):
    return jax.shard_map(
        on_device,
        mesh=mesh,
        in_specs=(
            P(("dp", "ctx", "head"), None),
            P(None, ("dp", "ctx", "head"), None),
            P(("dp", "ctx", "head"), None),
            P(None, ("dp", "ctx", "head"), None),
            P(("dp", "ctx", "head"), None),
        ),
        out_specs=(P(("dp", "ctx", "head"), None), P(("dp", "ctx", "head"), None)),
        check_vma=False,
    )
```

```python
import functools
import math

import jax
import jax.numpy as jnp
from jax import lax
from jax.experimental import pallas as pl
from jax.experimental.pallas import tpu as pltpu
from jax.sharding import PartitionSpec as P

QUERY_HEAD_COUNT = 64
KEY_VALUE_HEADS = 8
HEAD_SIZE = 128
GROUP = QUERY_HEAD_COUNT // KEY_VALUE_HEADS
WIDE = GROUP * HEAD_SIZE

NEG_LARGE = -1e30
LOG2_SCALE = math.log2(math.e) / math.sqrt(HEAD_SIZE)

SIDE = 4
LOCAL_HEADS = KEY_VALUE_HEADS // 2
PAIR = LOCAL_HEADS // 2
PAIR_WIDTH = PAIR * HEAD_SIZE
MESH = pl.DeviceIdType.MESH

NEAR, FAR, RESULT, COPIES = 3, 11, 43, 45


def dot_nt(a, b):
    return lax.dot_general(a, b, (((1,), (1,)), ((), ())), preferred_element_type=jnp.float32)


def wrap(x):
    return lax.rem(x + SIDE, SIDE)


def order_of(index, half, core):
    return jnp.where(index < half, core * half + index, (1 - core) * half + index - half)


def kernel(
    q_hbm, kv_hbm, short_q_hbm, short_kv_hbm, seg, out_hbm, short_out_hbm,
    q, kv, acc, high, total, result, short_q, short_kv, send, recv, local,
):
    half = q_hbm.shape[0]
    rows = 2 * half
    ctx, head = lax.axis_index("ctx"), lax.axis_index("head")
    y, z, core = lax.div(ctx, 2), lax.rem(ctx, 2) * 2 + lax.div(head, 2), lax.rem(head, 2)
    chip = y * SIDE + z
    q_columns = LOCAL_HEADS * WIDE

    def device(to_y, to_z, to_core):
        return {"ctx": to_y * 2 + lax.div(to_z, 2), "head": lax.rem(to_z, 2) * 2 + to_core}

    mate = device(y, z, 1 - core)
    ahead = (device(y, wrap(z + 1), core), device(wrap(y + 1), z, core))
    behind = (device(y, wrap(z - 1), core), device(wrap(y - 1), z, core))

    def remote(src, dst, index, target):
        return pltpu.make_async_remote_copy(
            src_ref=src, dst_ref=dst, send_sem=send.at[index], recv_sem=recv.at[index], device_id=target, device_id_type=MESH
        )

    def mine_columns(side, of_core):
        start = of_core * (LOCAL_HEADS * HEAD_SIZE) + side * PAIR_WIDTH
        return pl.ds(pl.multiple_of(start, PAIR_WIDTH), PAIR_WIDTH)

    def heads_of(of_core, start, size):
        return pl.ds(pl.multiple_of(of_core * q_columns + start, size), size)

    def mate_kv(side):
        return remote(kv_hbm.at[:, :, mine_columns(side, 1 - core)], kv.at[side, 0, :, 0, pl.ds(half, half)], 1 + side, mate)

    def mate_q():
        return remote(q_hbm.at[:, heads_of(1 - core, 0, q_columns)], q.at[1], 0, mate)

    def near(side, which):
        index = NEAR + 4 * side + which
        if which == 0:
            return remote(kv.at[side, 0, :, 0], kv.at[side, 0, :, 1], index, ahead[side])
        if which == 1:
            return remote(kv.at[side, 0, :, 0], kv.at[side, 0, :, 2], index, behind[side])
        if which == 2:
            return remote(kv.at[side, 0, 0, 1], kv.at[side, 0, 0, 3], index, ahead[side])
        return remote(kv.at[side, 0, 1, 2], kv.at[side, 0, 1, 3], index, behind[side])

    def from_behind(side, piece, at_y):
        both = jnp.logical_or(side == 1, at_y == SIDE - 1)
        return jnp.where(both, 1 + piece // 2, 1), jnp.where(both, 2 * (piece % 2), piece)

    def from_ahead(side, piece, at_y):
        both = jnp.logical_or(side == 1, at_y == SIDE - 1)
        return jnp.where(both, 1 + piece // 2, 2), jnp.where(both, 2 * (piece % 2) + 1, piece)

    def far(side, piece, which):
        index = FAR + 16 * side + 4 * piece + which
        if which == 0:
            unit, slot = from_behind(side, piece, wrap(y + 1))
            return remote(kv.at[side, 0, :, piece], kv.at[side, unit, :, slot], index, ahead[1 - side])
        if which == 1:
            unit, slot = from_ahead(side, piece, wrap(y - 1))
            return remote(kv.at[side, 0, :, piece], kv.at[side, unit, :, slot], index, behind[1 - side])
        if which == 2:
            unit, slot = from_behind(side, piece, y)
            return remote(kv.at[side, unit, 0, slot], kv.at[side, 3, 0, piece], index, ahead[1 - side])
        unit, slot = from_ahead(side, piece, y)
        return remote(kv.at[side, unit, 1, slot], kv.at[side, 3, 1, piece], index, behind[1 - side])

    def give_back(side):
        columns = heads_of(core, side * (PAIR * WIDE), PAIR * WIDE)
        return remote(result.at[1, side], out_hbm.at[:, columns], RESULT + side, mate)

    def keep(side):
        columns = heads_of(core, side * (PAIR * WIDE), PAIR * WIDE)
        return pltpu.make_async_copy(result.at[0, side], out_hbm.at[:, columns], local.at[5 + side])

    own_q = pltpu.make_async_copy(q_hbm.at[:, heads_of(core, 0, q_columns)], q.at[0], local.at[0])
    own_kv = [
        pltpu.make_async_copy(kv_hbm.at[:, :, mine_columns(side, core)], kv.at[side, 0, :, 0, pl.ds(0, half)], local.at[1 + side])
        for side in range(2)
    ]
    get_short_q = pltpu.make_async_copy(short_q_hbm, short_q, local.at[3])
    get_short_kv = pltpu.make_async_copy(short_kv_hbm, short_kv, local.at[4])
    put_short = pltpu.make_async_copy(short_q, short_out_hbm, local.at[7])

    own_kv[0].start()
    own_kv[1].start()
    barrier = pltpu.get_barrier_semaphore()
    for target in (mate,) + ahead + behind:
        pl.semaphore_signal(barrier, inc=1, device_id=target, device_id_type=MESH)
    pl.semaphore_wait(barrier, 5)
    for side in range(2):
        mate_kv(side).start()
    mate_q().start()
    get_short_kv.start()
    get_short_q.start()
    own_q.start()
    for side in range(2):
        own_kv[side].wait()
        mate_kv(side).wait_recv()
        near(side, 0).start()
        near(side, 1).start()
    for side in range(2):
        far(side, 0, 0).start()
        far(side, 0, 1).start()

    tokens = short_q.shape[0]
    part_rows = tokens // 2
    seg_row = seg[...].astype(jnp.float32)
    seg_col = jnp.broadcast_to(seg_row, (HEAD_SIZE, tokens)).T

    def short_head(g, carry):
        key_columns = pl.ds(pl.multiple_of(g * HEAD_SIZE, HEAD_SIZE), HEAD_SIZE)
        k, v = short_kv[0, :, key_columns], short_kv[1, :, key_columns]
        v_one = jnp.concatenate([v, jnp.ones_like(v)], axis=1)
        columns = [pl.ds(pl.multiple_of(g * WIDE + h * HEAD_SIZE, HEAD_SIZE), HEAD_SIZE) for h in range(GROUP)]
        for part in range(2):
            low, keys = part * part_rows, (part + 1) * part_rows
            q_pos = low + lax.broadcasted_iota(jnp.int32, (part_rows, keys), 0)
            k_pos = lax.broadcasted_iota(jnp.int32, (part_rows, keys), 1)
            same = seg_col[low : low + part_rows, :1] == seg_row[:1, :keys]
            allowed = (k_pos <= q_pos) & same
            weights = []
            for s in [dot_nt(short_q[low : low + part_rows, c], k[:keys]) for c in columns]:
                s = jnp.where(allowed, s, NEG_LARGE)
                top = jnp.max(s, axis=1, keepdims=True)
                weights.append(jnp.exp2((s - top) * LOG2_SCALE).astype(jnp.bfloat16))
            mixes = [jnp.dot(p, v_one[:keys], preferred_element_type=jnp.float32) for p in weights]
            for c, mixed in zip(columns, mixes):
                short_q[low : low + part_rows, c] = (mixed[:, :HEAD_SIZE] / mixed[:, HEAD_SIZE:]).astype(jnp.bfloat16)
        return carry

    get_short_kv.wait()
    get_short_q.wait()

    def short_step(g, carry):
        short_head(g, carry)

        @pl.when(g == 5)
        def _():
            for side in range(2):
                near(side, 0).wait_recv()
                near(side, 2).start()
                near(side, 1).wait_recv()
                near(side, 3).start()
            for piece in (1, 2):
                for side in range(2):
                    far(side, piece, 0).start()
                    far(side, piece, 1).start()

        return carry

    lax.fori_loop(0, KEY_VALUE_HEADS, short_step, 0)
    put_short.start()
    own_q.wait()
    mate_q().wait_recv()
    for side in range(2):
        near(side, 2).wait_recv()
        near(side, 3).wait_recv()
        far(side, 3, 0).start()
        far(side, 3, 1).start()

    q_pos = chip * rows + order_of(lax.broadcasted_iota(jnp.int32, (rows, 1), 0), half, core)
    key_index = order_of(lax.broadcasted_iota(jnp.int32, (1, rows), 1), half, core)

    def phase(number, carry):
        unit, side = lax.div(number, 2), lax.rem(number, 2)
        owners = []
        for slot in range(SIDE):
            both = jnp.logical_or(side == 1, y == SIDE - 1)
            beyond = jnp.where(both, slot // 2 + 2 * (unit - 1), slot)
            ring = jnp.where(jnp.logical_or(unit == 0, unit == 3), slot, beyond)
            next_to = jnp.where(both, 2 * (slot % 2) - 1, 2 * unit - 3)
            along = jnp.where(ring == 1, -1, jnp.where(ring == 2, 1, jnp.where(ring == 3, 2, 0)))
            across = jnp.where(unit == 0, 0, jnp.where(unit == 3, 2, next_to))
            owner_y = wrap(y + jnp.where(side == 0, across, along))
            owner_z = wrap(z + jnp.where(side == 0, along, across))
            owners.append(owner_y * SIDE + owner_z)
        low = jnp.minimum(jnp.minimum(owners[0], owners[1]), jnp.minimum(owners[2], owners[3]))
        top = jnp.maximum(jnp.maximum(owners[0], owners[1]), jnp.maximum(owners[2], owners[3]))

        def block(local_head, plane):
            columns = pl.ds(pl.multiple_of(local_head * HEAD_SIZE, HEAD_SIZE), HEAD_SIZE)
            return kv[side, unit, plane, :, :, columns].reshape(SIDE * rows, HEAD_SIZE)

        def scores(item, k):
            columns = pl.ds(pl.multiple_of((side * PAIR * GROUP + item) * HEAD_SIZE, HEAD_SIZE), HEAD_SIZE)
            query = jnp.concatenate([q[0, :, columns], q[1, :, columns]], axis=0)
            return dot_nt(query, k)

        def update(item, s, v_one, masked, first):
            if masked:
                k_pos = jnp.concatenate([owner * rows + key_index for owner in owners], axis=1)
                s = jnp.where(k_pos <= q_pos, s, NEG_LARGE)
            r = pl.ds(pl.multiple_of((side * PAIR * GROUP + item) * rows, rows), rows)
            best = jnp.max(s, axis=1, keepdims=True) * LOG2_SCALE
            if first:
                new = jnp.broadcast_to(best, (rows, HEAD_SIZE))
            else:
                old = high[r, :]
                new = jnp.maximum(old, best)
                factor = jnp.exp2(old - new)
            p = jnp.exp2(s * LOG2_SCALE - new[:, :1]).astype(jnp.bfloat16)
            mixed = jnp.dot(p, v_one, preferred_element_type=jnp.float32)
            high[r, :] = new
            if first:
                acc[r, :] = mixed[:, :HEAD_SIZE]
                total[r, :] = mixed[:, HEAD_SIZE:]
            else:
                acc[r, :] = acc[r, :] * factor + mixed[:, :HEAD_SIZE]
                total[r, :] = total[r, :] * factor + mixed[:, HEAD_SIZE:]

        def run(masked, first):
            def one_head(local_head, inner):
                k, v = block(local_head, 0), block(local_head, 1)
                v_one = jnp.concatenate([v, jnp.ones_like(v)], axis=1)
                start = local_head * GROUP
                s = scores(start, k)
                for h in range(GROUP):
                    ahead_s = scores(start + h + 1, k) if h + 1 < GROUP else None
                    update(start + h, s, v_one, masked, first)
                    s = ahead_s
                return inner

            lax.fori_loop(0, PAIR, one_head, 0)

        @pl.when(unit == 0)
        def _():
            run(True, True)

        used = jnp.logical_and(unit > 0, low <= chip)

        @pl.when(jnp.logical_and(used, top < chip))
        def _():
            run(False, False)

        @pl.when(jnp.logical_and(used, top >= chip))
        def _():
            run(True, False)

        def pass_on(pieces):
            for piece in pieces:
                for side in range(2):
                    far(side, piece, 0).wait_recv()
                    far(side, piece, 2).start()
                    far(side, piece, 1).wait_recv()
                    far(side, piece, 3).start()

        @pl.when(number == 0)
        def _():
            pass_on((0,))

        @pl.when(number == 1)
        def _():
            pass_on((1,))

        @pl.when(number == jnp.where(y == SIDE - 1, 3, 1))
        def _():
            pass_on((2, 3))

        @pl.when(number == 5)
        def _():
            for piece in range(SIDE):
                for side in range(2):
                    far(side, piece, 2).wait_recv()
                    far(side, piece, 3).wait_recv()

        @pl.when(unit == 3)
        def _():
            def divide(item, inner):
                r = pl.multiple_of((side * PAIR * GROUP + item) * rows, rows)
                columns = pl.ds(pl.multiple_of(item * HEAD_SIZE, HEAD_SIZE), HEAD_SIZE)
                for who in range(2):
                    part = pl.ds(r + who * half, half)
                    result[who, side, :, columns] = (acc[part, :] / total[part, :]).astype(jnp.bfloat16)
                return inner

            lax.fori_loop(0, PAIR * GROUP, divide, 0)

        for of_side in range(2):

            @pl.when(number == 6 + of_side)
            def _(of_side=of_side):
                give_back(of_side).start()
                keep(of_side).start()

        return carry

    lax.fori_loop(0, 8, phase, 0)

    put_short.wait()
    for side in range(2):
        keep(side).wait()
        give_back(side).wait_recv()
        give_back(side).wait_send()
        mate_kv(side).wait_send()
        for which in range(4):
            near(side, which).wait_send()
            for piece in range(SIDE):
                far(side, piece, which).wait_send()
    mate_q().wait_send()


def on_device(long_query, long_kv, short_query, short_key_value, short_seg):
    half = long_query.shape[0]
    rows = 2 * half
    state_rows = LOCAL_HEADS * GROUP * rows
    anywhere = pl.BlockSpec(memory_space=pl.ANY)
    vmem = pl.BlockSpec(memory_space=pltpu.VMEM)
    return pl.pallas_call(
        kernel,
        out_shape=(
            jax.ShapeDtypeStruct(long_query.shape, long_query.dtype),
            jax.ShapeDtypeStruct(short_query.shape, short_query.dtype),
        ),
        in_specs=[anywhere] * 4 + [vmem],
        out_specs=(anywhere, anywhere),
        scratch_shapes=[
            pltpu.VMEM((2, half, LOCAL_HEADS * WIDE), jnp.bfloat16),
            pltpu.VMEM((2, 4, 2, SIDE, rows, PAIR_WIDTH), jnp.bfloat16),
            pltpu.VMEM((state_rows, HEAD_SIZE), jnp.float32),
            pltpu.VMEM((state_rows, HEAD_SIZE), jnp.float32),
            pltpu.VMEM((state_rows, HEAD_SIZE), jnp.float32),
            pltpu.VMEM((2, 2, half, PAIR * WIDE), jnp.bfloat16),
            pltpu.VMEM(short_query.shape, jnp.bfloat16),
            pltpu.VMEM(short_key_value.shape, jnp.bfloat16),
            pltpu.SemaphoreType.DMA((COPIES,)),
            pltpu.SemaphoreType.DMA((COPIES,)),
            pltpu.SemaphoreType.DMA((8,)),
        ],
        compiler_params=pltpu.CompilerParams(
            collective_id=0, has_side_effects=True, vmem_limit_bytes=63 << 20
        ),
        name="window_attention",
    )(long_query, long_kv, short_query, short_key_value, short_seg)


def solution(mesh):
    return jax.shard_map(
        on_device,
        mesh=mesh,
        in_specs=(
            P(("dp", "ctx", "head"), None),
            P(None, ("dp", "ctx", "head"), None),
            P(("dp", "ctx", "head"), None),
            P(None, ("dp", "ctx", "head"), None),
            P(("dp", "ctx", "head"), None),
        ),
        out_specs=(P(("dp", "ctx", "head"), None), P(("dp", "ctx", "head"), None)),
        check_vma=False,
    )
```

```python
import functools
import math

import jax
import jax.numpy as jnp
from jax import lax
from jax.experimental import pallas as pl
from jax.experimental.pallas import tpu as pltpu
from jax.sharding import PartitionSpec as P

QUERY_HEAD_COUNT = 64
KEY_VALUE_HEADS = 8
HEAD_SIZE = 128
GROUP = QUERY_HEAD_COUNT // KEY_VALUE_HEADS
WIDE = GROUP * HEAD_SIZE

NEG_LARGE = -1e30
LOG2_SCALE = math.log2(math.e) / math.sqrt(HEAD_SIZE)

SIDE = 4
LOCAL_HEADS = KEY_VALUE_HEADS // 2
PAIR = LOCAL_HEADS // 2
PAIR_WIDTH = PAIR * HEAD_SIZE
MESH = pl.DeviceIdType.MESH

NEAR, FAR, RESULT, COPIES = 3, 11, 43, 45


def dot_nt(a, b):
    return lax.dot_general(a, b, (((1,), (1,)), ((), ())), preferred_element_type=jnp.float32)


def wrap(x):
    return lax.rem(x + SIDE, SIDE)


def order_of(index, half, core):
    return jnp.where(index < half, core * half + index, (1 - core) * half + index - half)


def kernel(
    q_hbm, kv_hbm, short_q_hbm, short_kv_hbm, seg, out_hbm, short_out_hbm,
    q, kv, acc, high, total, result, short_q, short_kv, send, recv, local,
):
    half = q_hbm.shape[0]
    rows = 2 * half
    ctx, head = lax.axis_index("ctx"), lax.axis_index("head")
    y, z, core = lax.div(ctx, 2), lax.rem(ctx, 2) * 2 + lax.div(head, 2), lax.rem(head, 2)
    chip = y * SIDE + z
    q_columns = LOCAL_HEADS * WIDE

    def device(to_y, to_z, to_core):
        return {"ctx": to_y * 2 + lax.div(to_z, 2), "head": lax.rem(to_z, 2) * 2 + to_core}

    mate = device(y, z, 1 - core)
    ahead = (device(y, wrap(z + 1), core), device(wrap(y + 1), z, core))
    behind = (device(y, wrap(z - 1), core), device(wrap(y - 1), z, core))

    def remote(src, dst, index, target):
        return pltpu.make_async_remote_copy(
            src_ref=src, dst_ref=dst, send_sem=send.at[index], recv_sem=recv.at[index], device_id=target, device_id_type=MESH
        )

    def mine_columns(side, of_core):
        start = of_core * (LOCAL_HEADS * HEAD_SIZE) + side * PAIR_WIDTH
        return pl.ds(pl.multiple_of(start, PAIR_WIDTH), PAIR_WIDTH)

    def heads_of(of_core, start, size):
        return pl.ds(pl.multiple_of(of_core * q_columns + start, size), size)

    def mate_kv(side):
        return remote(kv_hbm.at[:, :, mine_columns(side, 1 - core)], kv.at[side, 0, :, 0, pl.ds(half, half)], 1 + side, mate)

    def mate_q():
        return remote(q_hbm.at[:, heads_of(1 - core, 0, q_columns)], q.at[1], 0, mate)

    def near(side, which):
        index = NEAR + 4 * side + which
        if which == 0:
            return remote(kv.at[side, 0, :, 0], kv.at[side, 0, :, 1], index, ahead[side])
        if which == 1:
            return remote(kv.at[side, 0, :, 0], kv.at[side, 0, :, 2], index, behind[side])
        if which == 2:
            return remote(kv.at[side, 0, 0, 1], kv.at[side, 0, 0, 3], index, ahead[side])
        return remote(kv.at[side, 0, 1, 2], kv.at[side, 0, 1, 3], index, behind[side])

    def from_behind(side, piece, at_y):
        both = jnp.logical_or(side == 1, at_y == SIDE - 1)
        return jnp.where(both, 1 + piece // 2, 1), jnp.where(both, 2 * (piece % 2), piece)

    def from_ahead(side, piece, at_y):
        both = jnp.logical_or(side == 1, at_y == SIDE - 1)
        return jnp.where(both, 1 + piece // 2, 2), jnp.where(both, 2 * (piece % 2) + 1, piece)

    def far(side, piece, which):
        index = FAR + 16 * side + 4 * piece + which
        if which == 0:
            unit, slot = from_behind(side, piece, wrap(y + 1))
            return remote(kv.at[side, 0, :, piece], kv.at[side, unit, :, slot], index, ahead[1 - side])
        if which == 1:
            unit, slot = from_ahead(side, piece, wrap(y - 1))
            return remote(kv.at[side, 0, :, piece], kv.at[side, unit, :, slot], index, behind[1 - side])
        if which == 2:
            unit, slot = from_behind(side, piece, y)
            return remote(kv.at[side, unit, 0, slot], kv.at[side, 3, 0, piece], index, ahead[1 - side])
        unit, slot = from_ahead(side, piece, y)
        return remote(kv.at[side, unit, 1, slot], kv.at[side, 3, 1, piece], index, behind[1 - side])

    def give_back(side):
        columns = heads_of(core, side * (PAIR * WIDE), PAIR * WIDE)
        return remote(result.at[1, side], out_hbm.at[:, columns], RESULT + side, mate)

    def keep(side):
        columns = heads_of(core, side * (PAIR * WIDE), PAIR * WIDE)
        return pltpu.make_async_copy(result.at[0, side], out_hbm.at[:, columns], local.at[5 + side])

    own_q = pltpu.make_async_copy(q_hbm.at[:, heads_of(core, 0, q_columns)], q.at[0], local.at[0])
    own_kv = [
        pltpu.make_async_copy(kv_hbm.at[:, :, mine_columns(side, core)], kv.at[side, 0, :, 0, pl.ds(0, half)], local.at[1 + side])
        for side in range(2)
    ]
    get_short_q = pltpu.make_async_copy(short_q_hbm, short_q, local.at[3])
    get_short_kv = pltpu.make_async_copy(short_kv_hbm, short_kv, local.at[4])
    put_short = pltpu.make_async_copy(short_q, short_out_hbm, local.at[7])

    own_kv[0].start()
    own_kv[1].start()
    get_short_kv.start()
    get_short_q.start()
    own_q.start()
    barrier = pltpu.get_barrier_semaphore()
    for target in (mate,) + ahead + behind:
        pl.semaphore_signal(barrier, inc=1, device_id=target, device_id_type=MESH)
    pl.semaphore_wait(barrier, 5)
    for side in range(2):
        mate_kv(side).start()
    mate_q().start()
    for side in range(2):
        own_kv[side].wait()
        mate_kv(side).wait_recv()
        near(side, 0).start()
        near(side, 1).start()
    tokens = short_q.shape[0]
    part_rows = tokens // 2
    seg_row = seg[...].astype(jnp.float32)
    seg_col = jnp.broadcast_to(seg_row, (HEAD_SIZE, tokens)).T

    def short_head(g, carry):
        key_columns = pl.ds(pl.multiple_of(g * HEAD_SIZE, HEAD_SIZE), HEAD_SIZE)
        k, v = short_kv[0, :, key_columns], short_kv[1, :, key_columns]
        v_one = jnp.concatenate([v, jnp.ones_like(v)], axis=1)
        columns = [pl.ds(pl.multiple_of(g * WIDE + h * HEAD_SIZE, HEAD_SIZE), HEAD_SIZE) for h in range(GROUP)]
        for part in range(2):
            low, keys = part * part_rows, (part + 1) * part_rows
            q_pos = low + lax.broadcasted_iota(jnp.int32, (part_rows, keys), 0)
            k_pos = lax.broadcasted_iota(jnp.int32, (part_rows, keys), 1)
            same = seg_col[low : low + part_rows, :1] == seg_row[:1, :keys]
            allowed = (k_pos <= q_pos) & same
            weights = []
            for s in [dot_nt(short_q[low : low + part_rows, c], k[:keys]) for c in columns]:
                s = jnp.where(allowed, s, NEG_LARGE)
                top = jnp.max(s, axis=1, keepdims=True)
                weights.append(jnp.exp2((s - top) * LOG2_SCALE).astype(jnp.bfloat16))
            mixes = [jnp.dot(p, v_one[:keys], preferred_element_type=jnp.float32) for p in weights]
            for c, mixed in zip(columns, mixes):
                short_q[low : low + part_rows, c] = (mixed[:, :HEAD_SIZE] / mixed[:, HEAD_SIZE:]).astype(jnp.bfloat16)
        return carry

    get_short_kv.wait()
    get_short_q.wait()

    def short_step(g, carry):
        short_head(g, carry)

        @pl.when(g == 5)
        def _():
            for side in range(2):
                near(side, 0).wait_recv()
                near(side, 2).start()
                near(side, 1).wait_recv()
                near(side, 3).start()
            for piece in (0, 1, 2):
                for side in range(2):
                    far(side, piece, 0).start()
                    far(side, piece, 1).start()

        return carry

    lax.fori_loop(0, KEY_VALUE_HEADS, short_step, 0)
    put_short.start()
    own_q.wait()
    mate_q().wait_recv()
    for side in range(2):
        near(side, 2).wait_recv()
        near(side, 3).wait_recv()
        far(side, 3, 0).start()
        far(side, 3, 1).start()

    q_pos = chip * rows + order_of(lax.broadcasted_iota(jnp.int32, (rows, 1), 0), half, core)
    key_index = order_of(lax.broadcasted_iota(jnp.int32, (1, rows), 1), half, core)

    def phase(number, carry):
        unit, side = lax.div(number, 2), lax.rem(number, 2)
        owners = []
        for slot in range(SIDE):
            both = jnp.logical_or(side == 1, y == SIDE - 1)
            beyond = jnp.where(both, slot // 2 + 2 * (unit - 1), slot)
            ring = jnp.where(jnp.logical_or(unit == 0, unit == 3), slot, beyond)
            next_to = jnp.where(both, 2 * (slot % 2) - 1, 2 * unit - 3)
            along = jnp.where(ring == 1, -1, jnp.where(ring == 2, 1, jnp.where(ring == 3, 2, 0)))
            across = jnp.where(unit == 0, 0, jnp.where(unit == 3, 2, next_to))
            owner_y = wrap(y + jnp.where(side == 0, across, along))
            owner_z = wrap(z + jnp.where(side == 0, along, across))
            owners.append(owner_y * SIDE + owner_z)
        low = jnp.minimum(jnp.minimum(owners[0], owners[1]), jnp.minimum(owners[2], owners[3]))
        top = jnp.maximum(jnp.maximum(owners[0], owners[1]), jnp.maximum(owners[2], owners[3]))

        def block(local_head, plane):
            columns = pl.ds(pl.multiple_of(local_head * HEAD_SIZE, HEAD_SIZE), HEAD_SIZE)
            return kv[side, unit, plane, :, :, columns].reshape(SIDE * rows, HEAD_SIZE)

        def scores(item, k):
            columns = pl.ds(pl.multiple_of((side * PAIR * GROUP + item) * HEAD_SIZE, HEAD_SIZE), HEAD_SIZE)
            query = jnp.concatenate([q[0, :, columns], q[1, :, columns]], axis=0)
            return dot_nt(query, k)

        def update(item, s, v_one, masked, first):
            if masked:
                k_pos = jnp.concatenate([owner * rows + key_index for owner in owners], axis=1)
                s = jnp.where(k_pos <= q_pos, s, NEG_LARGE)
            r = pl.ds(pl.multiple_of((side * PAIR * GROUP + item) * rows, rows), rows)
            best = jnp.max(s, axis=1, keepdims=True) * LOG2_SCALE
            if first:
                new = jnp.broadcast_to(best, (rows, HEAD_SIZE))
            else:
                old = high[r, :]
                new = jnp.maximum(old, best)
                factor = jnp.exp2(old - new)
            p = jnp.exp2(s * LOG2_SCALE - new[:, :1]).astype(jnp.bfloat16)
            mixed = jnp.dot(p, v_one, preferred_element_type=jnp.float32)
            high[r, :] = new
            if first:
                acc[r, :] = mixed[:, :HEAD_SIZE]
                total[r, :] = mixed[:, HEAD_SIZE:]
            else:
                acc[r, :] = acc[r, :] * factor + mixed[:, :HEAD_SIZE]
                total[r, :] = total[r, :] * factor + mixed[:, HEAD_SIZE:]

        def run(masked, first):
            def some_heads(turn, inner):
                count = GROUP if masked else PAIR * GROUP
                start = turn * GROUP
                s = scores(start, block(turn, 0))
                for h in range(count):
                    local_head = turn + h // GROUP
                    following = turn + (h + 1) // GROUP
                    ahead_s = scores(start + h + 1, block(following, 0)) if h + 1 < count else None
                    v = block(local_head, 1)
                    update(start + h, s, jnp.concatenate([v, jnp.ones_like(v)], axis=1), masked, first)
                    s = ahead_s
                return inner

            if masked:
                lax.fori_loop(0, PAIR, some_heads, 0)
            else:
                some_heads(0, 0)

        @pl.when(unit == 0)
        def _():
            run(True, True)

        used = jnp.logical_and(unit > 0, low <= chip)

        @pl.when(jnp.logical_and(used, top < chip))
        def _():
            run(False, False)

        @pl.when(jnp.logical_and(used, top >= chip))
        def _():
            run(True, False)

        def pass_on(pieces):
            for piece in pieces:
                for side in range(2):
                    far(side, piece, 0).wait_recv()
                    far(side, piece, 2).start()
                    far(side, piece, 1).wait_recv()
                    far(side, piece, 3).start()

        @pl.when(number == 0)
        def _():
            pass_on((0,))

        @pl.when(number == 1)
        def _():
            pass_on((1,))

        @pl.when(number == jnp.where(y == SIDE - 1, 3, 1))
        def _():
            pass_on((2, 3))

        @pl.when(number == 5)
        def _():
            for piece in range(SIDE):
                for side in range(2):
                    far(side, piece, 2).wait_recv()
                    far(side, piece, 3).wait_recv()

        @pl.when(unit == 3)
        def _():
            def divide(item, inner):
                r = pl.multiple_of((side * PAIR * GROUP + item) * rows, rows)
                columns = pl.ds(pl.multiple_of(item * HEAD_SIZE, HEAD_SIZE), HEAD_SIZE)
                for who in range(2):
                    part = pl.ds(r + who * half, half)
                    result[who, side, :, columns] = (acc[part, :] / total[part, :]).astype(jnp.bfloat16)
                return inner

            lax.fori_loop(0, PAIR * GROUP, divide, 0)

        for of_side in range(2):

            @pl.when(number == 6 + of_side)
            def _(of_side=of_side):
                give_back(of_side).start()
                keep(of_side).start()

        return carry

    lax.fori_loop(0, 8, phase, 0)

    put_short.wait()
    for side in range(2):
        keep(side).wait()
        give_back(side).wait_recv()
        give_back(side).wait_send()
        mate_kv(side).wait_send()
        for which in range(4):
            near(side, which).wait_send()
            for piece in range(SIDE):
                far(side, piece, which).wait_send()
    mate_q().wait_send()


def on_device(long_query, long_kv, short_query, short_key_value, short_seg):
    half = long_query.shape[0]
    rows = 2 * half
    state_rows = LOCAL_HEADS * GROUP * rows
    anywhere = pl.BlockSpec(memory_space=pl.ANY)
    vmem = pl.BlockSpec(memory_space=pltpu.VMEM)
    return pl.pallas_call(
        kernel,
        out_shape=(
            jax.ShapeDtypeStruct(long_query.shape, long_query.dtype),
            jax.ShapeDtypeStruct(short_query.shape, short_query.dtype),
        ),
        in_specs=[anywhere] * 4 + [vmem],
        out_specs=(anywhere, anywhere),
        scratch_shapes=[
            pltpu.VMEM((2, half, LOCAL_HEADS * WIDE), jnp.bfloat16),
            pltpu.VMEM((2, 4, 2, SIDE, rows, PAIR_WIDTH), jnp.bfloat16),
            pltpu.VMEM((state_rows, HEAD_SIZE), jnp.float32),
            pltpu.VMEM((state_rows, HEAD_SIZE), jnp.float32),
            pltpu.VMEM((state_rows, HEAD_SIZE), jnp.float32),
            pltpu.VMEM((2, 2, half, PAIR * WIDE), jnp.bfloat16),
            pltpu.VMEM(short_query.shape, jnp.bfloat16),
            pltpu.VMEM(short_key_value.shape, jnp.bfloat16),
            pltpu.SemaphoreType.DMA((COPIES,)),
            pltpu.SemaphoreType.DMA((COPIES,)),
            pltpu.SemaphoreType.DMA((8,)),
        ],
        compiler_params=pltpu.CompilerParams(
            collective_id=0, has_side_effects=True, vmem_limit_bytes=63 << 20
        ),
        name="window_attention",
    )(long_query, long_kv, short_query, short_key_value, short_seg)


def solution(mesh):
    return jax.shard_map(
        on_device,
        mesh=mesh,
        in_specs=(
            P(("dp", "ctx", "head"), None),
            P(None, ("dp", "ctx", "head"), None),
            P(("dp", "ctx", "head"), None),
            P(None, ("dp", "ctx", "head"), None),
            P(("dp", "ctx", "head"), None),
        ),
        out_specs=(P(("dp", "ctx", "head"), None), P(("dp", "ctx", "head"), None)),
        check_vma=False,
    )
```

```python
import functools
import math

import jax
import jax.numpy as jnp
from jax import lax
from jax.experimental import pallas as pl
from jax.experimental.pallas import tpu as pltpu
from jax.sharding import PartitionSpec as P

QUERY_HEAD_COUNT = 64
KEY_VALUE_HEADS = 8
HEAD_SIZE = 128
GROUP = QUERY_HEAD_COUNT // KEY_VALUE_HEADS
WIDE = GROUP * HEAD_SIZE

NEG_LARGE = -1e30
LOG2_SCALE = math.log2(math.e) / math.sqrt(HEAD_SIZE)

SIDE = 4
LOCAL_HEADS = KEY_VALUE_HEADS // 2
PAIR = LOCAL_HEADS // 2
PAIR_WIDTH = PAIR * HEAD_SIZE
MESH = pl.DeviceIdType.MESH

NEAR, FAR, RESULT, SHARE, COPIES = 3, 11, 43, 45, 48

SHARED = 4
KEPT = PAIR * GROUP - SHARED


def dot_nt(a, b):
    return lax.dot_general(a, b, (((1,), (1,)), ((), ())), preferred_element_type=jnp.float32)


def wrap(x):
    return lax.rem(x + SIDE, SIDE)


def order_of(index, half, core):
    return jnp.where(index < half, core * half + index, (1 - core) * half + index - half)


def kernel(
    q_hbm, kv_hbm, short_q_hbm, short_kv_hbm, seg, out_hbm, short_out_hbm,
    q, kv, acc, high, total, result, q_extra, result_extra, short_q, short_kv, send, recv, local,
):
    half = q_hbm.shape[0]
    rows = 2 * half
    ctx, head = lax.axis_index("ctx"), lax.axis_index("head")
    y, z, core = lax.div(ctx, 2), lax.rem(ctx, 2) * 2 + lax.div(head, 2), lax.rem(head, 2)
    chip = y * SIDE + z
    q_columns = LOCAL_HEADS * WIDE

    def device(to_y, to_z, to_core):
        return {"ctx": to_y * 2 + lax.div(to_z, 2), "head": lax.rem(to_z, 2) * 2 + to_core}

    mate = device(y, z, 1 - core)
    ahead = (device(y, wrap(z + 1), core), device(wrap(y + 1), z, core))
    behind = (device(y, wrap(z - 1), core), device(wrap(y - 1), z, core))

    def remote(src, dst, index, target):
        return pltpu.make_async_remote_copy(
            src_ref=src, dst_ref=dst, send_sem=send.at[index], recv_sem=recv.at[index], device_id=target, device_id_type=MESH
        )

    def mine_columns(side, of_core):
        start = of_core * (LOCAL_HEADS * HEAD_SIZE) + side * PAIR_WIDTH
        return pl.ds(pl.multiple_of(start, PAIR_WIDTH), PAIR_WIDTH)

    def heads_of(of_core, start, size):
        return pl.ds(pl.multiple_of(of_core * q_columns + start, SHARED * HEAD_SIZE), size)

    def mate_kv(side):
        return remote(kv_hbm.at[:, :, mine_columns(side, 1 - core)], kv.at[side, 0, :, 0, pl.ds(half, half)], 1 + side, mate)

    def mate_q():
        return remote(q_hbm.at[:, heads_of(1 - core, 0, q_columns)], q.at[1], 0, mate)

    def near(side, which):
        index = NEAR + 4 * side + which
        if which == 0:
            return remote(kv.at[side, 0, :, 0], kv.at[side, 0, :, 1], index, ahead[side])
        if which == 1:
            return remote(kv.at[side, 0, :, 0], kv.at[side, 0, :, 2], index, behind[side])
        if which == 2:
            return remote(kv.at[side, 0, 0, 1], kv.at[side, 0, 0, 3], index, ahead[side])
        return remote(kv.at[side, 0, 1, 2], kv.at[side, 0, 1, 3], index, behind[side])

    def from_behind(side, piece, at_y):
        both = jnp.logical_or(side == 1, at_y == SIDE - 1)
        return jnp.where(both, 1 + piece // 2, 1), jnp.where(both, 2 * (piece % 2), piece)

    def from_ahead(side, piece, at_y):
        both = jnp.logical_or(side == 1, at_y == SIDE - 1)
        return jnp.where(both, 1 + piece // 2, 2), jnp.where(both, 2 * (piece % 2) + 1, piece)

    def far(side, piece, which):
        index = FAR + 16 * side + 4 * piece + which
        if which == 0:
            unit, slot = from_behind(side, piece, wrap(y + 1))
            return remote(kv.at[side, 0, :, piece], kv.at[side, unit, :, slot], index, ahead[1 - side])
        if which == 1:
            unit, slot = from_ahead(side, piece, wrap(y - 1))
            return remote(kv.at[side, 0, :, piece], kv.at[side, unit, :, slot], index, behind[1 - side])
        if which == 2:
            unit, slot = from_behind(side, piece, y)
            return remote(kv.at[side, unit, 0, slot], kv.at[side, 3, 0, piece], index, ahead[1 - side])
        unit, slot = from_ahead(side, piece, y)
        return remote(kv.at[side, unit, 1, slot], kv.at[side, 3, 1, piece], index, behind[1 - side])

    def give_back(side, width):
        columns = heads_of(core, side * (PAIR * WIDE), width)
        return remote(result.at[1, side, :, pl.ds(0, width)], out_hbm.at[:, columns], RESULT + side, mate)

    def keep(side, width):
        columns = heads_of(core, side * (PAIR * WIDE), width)
        return pltpu.make_async_copy(result.at[0, side, :, pl.ds(0, width)], out_hbm.at[:, columns], local.at[5 + side])

    gives, takes = y == SIDE - 1, y == 0
    whole, part_width = PAIR * WIDE, KEPT * HEAD_SIZE

    def share_q():
        return remote(q.at[:, :, pl.ds(part_width, SHARED * HEAD_SIZE)], q_extra, SHARE, ahead[1])

    def share_result(who):
        columns = heads_of(core, part_width, SHARED * HEAD_SIZE)
        target = behind[1] if who == 0 else device(wrap(y - 1), z, 1 - core)
        return remote(result_extra.at[who], out_hbm.at[:, columns], SHARE + 1 + who, target)

    own_q = pltpu.make_async_copy(q_hbm.at[:, heads_of(core, 0, q_columns)], q.at[0], local.at[0])
    own_kv = [
        pltpu.make_async_copy(kv_hbm.at[:, :, mine_columns(side, core)], kv.at[side, 0, :, 0, pl.ds(0, half)], local.at[1 + side])
        for side in range(2)
    ]
    get_short_q = pltpu.make_async_copy(short_q_hbm, short_q, local.at[3])
    get_short_kv = pltpu.make_async_copy(short_kv_hbm, short_kv, local.at[4])
    put_short = pltpu.make_async_copy(short_q, short_out_hbm, local.at[7])

    own_kv[0].start()
    own_kv[1].start()
    get_short_kv.start()
    get_short_q.start()
    own_q.start()
    barrier = pltpu.get_barrier_semaphore()
    crossed = (device(wrap(y + 1), z, 1 - core), device(wrap(y - 1), z, 1 - core))
    for target in (mate,) + ahead + behind + crossed:
        pl.semaphore_signal(barrier, inc=1, device_id=target, device_id_type=MESH)
    pl.semaphore_wait(barrier, 7)
    for side in range(2):
        mate_kv(side).start()
    mate_q().start()
    for side in range(2):
        own_kv[side].wait()
        mate_kv(side).wait_recv()
        near(side, 0).start()
        near(side, 1).start()
    tokens = short_q.shape[0]
    part_rows = tokens // 2
    seg_row = seg[...].astype(jnp.float32)
    seg_col = jnp.broadcast_to(seg_row, (HEAD_SIZE, tokens)).T

    def short_head(g, carry):
        key_columns = pl.ds(pl.multiple_of(g * HEAD_SIZE, HEAD_SIZE), HEAD_SIZE)
        k, v = short_kv[0, :, key_columns], short_kv[1, :, key_columns]
        v_one = jnp.concatenate([v, jnp.ones_like(v)], axis=1)
        columns = [pl.ds(pl.multiple_of(g * WIDE + h * HEAD_SIZE, HEAD_SIZE), HEAD_SIZE) for h in range(GROUP)]
        for part in range(2):
            low, keys = part * part_rows, (part + 1) * part_rows
            q_pos = low + lax.broadcasted_iota(jnp.int32, (part_rows, keys), 0)
            k_pos = lax.broadcasted_iota(jnp.int32, (part_rows, keys), 1)
            same = seg_col[low : low + part_rows, :1] == seg_row[:1, :keys]
            allowed = (k_pos <= q_pos) & same
            weights = []
            for s in [dot_nt(short_q[low : low + part_rows, c], k[:keys]) for c in columns]:
                s = jnp.where(allowed, s, NEG_LARGE)
                top = jnp.max(s, axis=1, keepdims=True)
                weights.append(jnp.exp2((s - top) * LOG2_SCALE).astype(jnp.bfloat16))
            mixes = [jnp.dot(p, v_one[:keys], preferred_element_type=jnp.float32) for p in weights]
            for c, mixed in zip(columns, mixes):
                short_q[low : low + part_rows, c] = (mixed[:, :HEAD_SIZE] / mixed[:, HEAD_SIZE:]).astype(jnp.bfloat16)
        return carry

    get_short_kv.wait()
    get_short_q.wait()

    def short_step(g, carry):
        short_head(g, carry)

        @pl.when(g == 5)
        def _():
            for side in range(2):
                near(side, 0).wait_recv()
                near(side, 2).start()
                near(side, 1).wait_recv()
                near(side, 3).start()
            for piece in (0, 1, 2):
                for side in range(2):
                    far(side, piece, 0).start()
                    far(side, piece, 1).start()

        return carry

    lax.fori_loop(0, KEY_VALUE_HEADS, short_step, 0)
    put_short.start()
    own_q.wait()
    mate_q().wait_recv()

    @pl.when(gives)
    def _():
        share_q().start()

    for side in range(2):
        near(side, 2).wait_recv()
        near(side, 3).wait_recv()
        far(side, 3, 0).start()
        far(side, 3, 1).start()

    q_pos = chip * rows + order_of(lax.broadcasted_iota(jnp.int32, (rows, 1), 0), half, core)
    key_index = order_of(lax.broadcasted_iota(jnp.int32, (1, rows), 1), half, core)

    def owners_of(unit, side):
        owners = []
        for slot in range(SIDE):
            both = jnp.logical_or(side == 1, y == SIDE - 1)
            beyond = jnp.where(both, slot // 2 + 2 * (unit - 1), slot)
            ring = jnp.where(jnp.logical_or(unit == 0, unit == 3), slot, beyond)
            next_to = jnp.where(both, 2 * (slot % 2) - 1, 2 * unit - 3)
            along = jnp.where(ring == 1, -1, jnp.where(ring == 2, 1, jnp.where(ring == 3, 2, 0)))
            across = jnp.where(unit == 0, 0, jnp.where(unit == 3, 2, next_to))
            owner_y = wrap(y + jnp.where(side == 0, across, along))
            owner_z = wrap(z + jnp.where(side == 0, along, across))
            owners.append(owner_y * SIDE + owner_z)
        return owners

    def phase(number, carry):
        unit = lax.div(number, 2)
        side = jnp.where(unit == 1, 1 - lax.rem(number, 2), lax.rem(number, 2))
        owners = owners_of(unit, side)
        low = jnp.minimum(jnp.minimum(owners[0], owners[1]), jnp.minimum(owners[2], owners[3]))
        top = jnp.maximum(jnp.maximum(owners[0], owners[1]), jnp.maximum(owners[2], owners[3]))

        def block(local_head, plane, of_side=side, of_unit=unit):
            columns = pl.ds(pl.multiple_of(local_head * HEAD_SIZE, HEAD_SIZE), HEAD_SIZE)
            return kv[of_side, of_unit, plane, :, :, columns].reshape(SIDE * rows, HEAD_SIZE)

        def scores(item, k):
            columns = pl.ds(pl.multiple_of((side * PAIR * GROUP + item) * HEAD_SIZE, HEAD_SIZE), HEAD_SIZE)
            query = jnp.concatenate([q[0, :, columns], q[1, :, columns]], axis=0)
            return dot_nt(query, k)

        def update(place, s, v, owners, positions, first):
            v_one = jnp.concatenate([v, jnp.ones_like(v)], axis=1)
            if owners is not None:
                k_pos = jnp.concatenate([owner * rows + key_index for owner in owners], axis=1)
                s = jnp.where(k_pos <= positions, s, NEG_LARGE)
            r = pl.ds(pl.multiple_of(place * rows, rows), rows)
            best = jnp.max(s, axis=1, keepdims=True) * LOG2_SCALE
            if first:
                new = jnp.broadcast_to(best, (rows, HEAD_SIZE))
            else:
                old = high[r, :]
                new = jnp.maximum(old, best)
                factor = jnp.exp2(old - new)
            p = jnp.exp2(s * LOG2_SCALE - new[:, :1]).astype(jnp.bfloat16)
            mixed = jnp.dot(p, v_one, preferred_element_type=jnp.float32)
            high[r, :] = new
            if first:
                acc[r, :] = mixed[:, :HEAD_SIZE]
                total[r, :] = mixed[:, HEAD_SIZE:]
            else:
                acc[r, :] = acc[r, :] * factor + mixed[:, :HEAD_SIZE]
                total[r, :] = total[r, :] * factor + mixed[:, HEAD_SIZE:]

        def run(masked, first, begin=0, straight=PAIR * GROUP):
            def some_heads(turn, inner):
                count = GROUP if masked else straight
                start = turn * GROUP + begin
                s = scores(start, block(turn + begin // GROUP, 0))
                for h in range(count):
                    local_head = turn + (begin + h) // GROUP
                    following = turn + (begin + h + 1) // GROUP
                    ahead_s = scores(start + h + 1, block(following, 0)) if h + 1 < count else None
                    place = side * PAIR * GROUP + start + h
                    update(place, s, block(local_head, 1), owners if masked else None, q_pos, first)
                    s = ahead_s
                return inner

            if masked:
                lax.fori_loop(0, PAIR, some_heads, 0)
            else:
                some_heads(0, 0)

        @pl.when(unit == 0)
        def _():
            run(True, True)

        used = jnp.logical_and(unit > 0, low <= chip)

        clear = jnp.logical_and(used, top < chip)
        fewer = jnp.logical_and(gives, side == 0)

        @pl.when(clear)
        def _():
            run(False, False, 0, KEPT)

        @pl.when(jnp.logical_and(clear, jnp.logical_not(fewer)))
        def _():
            run(False, False, KEPT, SHARED)

        @pl.when(jnp.logical_and(used, top >= chip))
        def _():
            run(True, False)

        def pass_on(pieces):
            for piece in pieces:
                for side in range(2):
                    far(side, piece, 0).wait_recv()
                    far(side, piece, 2).start()
                    far(side, piece, 1).wait_recv()
                    far(side, piece, 3).start()

        @pl.when(number == 0)
        def _():
            pass_on((0,))

        @pl.when(number == 1)
        def _():
            pass_on((1,))

        @pl.when(number == jnp.where(y == SIDE - 1, 3, 2))
        def _():
            pass_on((2, 3))

        @pl.when(number == 5)
        def _():
            for piece in range(SIDE):
                for side in range(2):
                    far(side, piece, 2).wait_recv()
                    far(side, piece, 3).wait_recv()

        extra = LOCAL_HEADS * GROUP

        @pl.when(jnp.logical_and(takes, number == 3))
        def _():
            share_q().wait_recv()
            area = pl.ds(extra * rows, SHARED * rows)
            acc[area, :] = jnp.zeros((SHARED * rows, HEAD_SIZE), jnp.float32)
            total[area, :] = jnp.zeros((SHARED * rows, HEAD_SIZE), jnp.float32)
            high[area, :] = jnp.full((SHARED * rows, HEAD_SIZE), NEG_LARGE, jnp.float32)

        @pl.when(jnp.logical_and(takes, jnp.logical_or(number == 3, number == 5)))
        def _():
            def shared_unit(of_unit, inner):
                local_head = KEPT // GROUP
                k, v = block(local_head, 0, 0, of_unit), block(local_head, 1, 0, of_unit)
                positions = q_pos + (SIDE - 1) * SIDE * rows
                for h in range(SHARED):
                    columns = slice(h * HEAD_SIZE, (h + 1) * HEAD_SIZE)
                    query = jnp.concatenate([q_extra[0, :, columns], q_extra[1, :, columns]], axis=0)
                    update(extra + h, dot_nt(query, k), v, owners_of(of_unit, 0), positions, False)
                return inner

            lax.fori_loop(jnp.where(number == 3, 0, 3), jnp.where(number == 3, 3, 4), shared_unit, 0)

        @pl.when(jnp.logical_and(takes, number == 5))
        def _():
            for h in range(SHARED):
                for who in range(2):
                    part = pl.ds((extra + h) * rows + who * half, half)
                    result_extra[who, :, h * HEAD_SIZE : (h + 1) * HEAD_SIZE] = (acc[part, :] / total[part, :]).astype(jnp.bfloat16)
            share_result(0).start()
            share_result(1).start()

        @pl.when(unit == 3)
        def _():
            def divide(item, inner):
                r = pl.multiple_of((side * PAIR * GROUP + item) * rows, rows)
                columns = pl.ds(pl.multiple_of(item * HEAD_SIZE, HEAD_SIZE), HEAD_SIZE)
                for who in range(2):
                    part = pl.ds(r + who * half, half)
                    result[who, side, :, columns] = (acc[part, :] / total[part, :]).astype(jnp.bfloat16)
                return inner

            lax.fori_loop(0, PAIR * GROUP, divide, 0)

        @pl.when(jnp.logical_and(number == 6, gives))
        def _():
            give_back(0, part_width).start()
            keep(0, part_width).start()

        @pl.when(jnp.logical_and(number == 6, jnp.logical_not(gives)))
        def _():
            give_back(0, whole).start()
            keep(0, whole).start()

        @pl.when(number == 7)
        def _():
            give_back(1, whole).start()
            keep(1, whole).start()

        return carry

    lax.fori_loop(0, 8, phase, 0)

    put_short.wait()
    def finish(side, width):
        keep(side, width).wait()
        give_back(side, width).wait_recv()
        give_back(side, width).wait_send()

    finish(1, whole)

    @pl.when(gives)
    def _():
        finish(0, part_width)
        share_q().wait_send()
        share_result(0).wait_recv()
        share_result(1).wait_recv()

    @pl.when(jnp.logical_not(gives))
    def _():
        finish(0, whole)

    @pl.when(takes)
    def _():
        share_result(0).wait_send()
        share_result(1).wait_send()

    for side in range(2):
        mate_kv(side).wait_send()
        for which in range(4):
            near(side, which).wait_send()
            for piece in range(SIDE):
                far(side, piece, which).wait_send()
    mate_q().wait_send()


def on_device(long_query, long_kv, short_query, short_key_value, short_seg):
    half = long_query.shape[0]
    rows = 2 * half
    state_rows = (LOCAL_HEADS * GROUP + SHARED) * rows
    anywhere = pl.BlockSpec(memory_space=pl.ANY)
    vmem = pl.BlockSpec(memory_space=pltpu.VMEM)
    return pl.pallas_call(
        kernel,
        out_shape=(
            jax.ShapeDtypeStruct(long_query.shape, long_query.dtype),
            jax.ShapeDtypeStruct(short_query.shape, short_query.dtype),
        ),
        in_specs=[anywhere] * 4 + [vmem],
        out_specs=(anywhere, anywhere),
        scratch_shapes=[
            pltpu.VMEM((2, half, LOCAL_HEADS * WIDE), jnp.bfloat16),
            pltpu.VMEM((2, 4, 2, SIDE, rows, PAIR_WIDTH), jnp.bfloat16),
            pltpu.VMEM((state_rows, HEAD_SIZE), jnp.float32),
            pltpu.VMEM((state_rows, HEAD_SIZE), jnp.float32),
            pltpu.VMEM((state_rows, HEAD_SIZE), jnp.float32),
            pltpu.VMEM((2, 2, half, PAIR * WIDE), jnp.bfloat16),
            pltpu.VMEM((2, half, SHARED * HEAD_SIZE), jnp.bfloat16),
            pltpu.VMEM((2, half, SHARED * HEAD_SIZE), jnp.bfloat16),
            pltpu.VMEM(short_query.shape, jnp.bfloat16),
            pltpu.VMEM(short_key_value.shape, jnp.bfloat16),
            pltpu.SemaphoreType.DMA((COPIES,)),
            pltpu.SemaphoreType.DMA((COPIES,)),
            pltpu.SemaphoreType.DMA((8,)),
        ],
        compiler_params=pltpu.CompilerParams(
            collective_id=0, has_side_effects=True, vmem_limit_bytes=63 << 20
        ),
        name="window_attention",
    )(long_query, long_kv, short_query, short_key_value, short_seg)


def solution(mesh):
    return jax.shard_map(
        on_device,
        mesh=mesh,
        in_specs=(
            P(("dp", "ctx", "head"), None),
            P(None, ("dp", "ctx", "head"), None),
            P(("dp", "ctx", "head"), None),
            P(None, ("dp", "ctx", "head"), None),
            P(("dp", "ctx", "head"), None),
        ),
        out_specs=(P(("dp", "ctx", "head"), None), P(("dp", "ctx", "head"), None)),
        check_vma=False,
    )
```

```python
import functools
import math

import jax
import jax.numpy as jnp
from jax import lax
from jax.experimental import pallas as pl
from jax.experimental.pallas import tpu as pltpu
from jax.sharding import PartitionSpec as P

QUERY_HEAD_COUNT = 64
KEY_VALUE_HEADS = 8
HEAD_SIZE = 128
GROUP = QUERY_HEAD_COUNT // KEY_VALUE_HEADS
WIDE = GROUP * HEAD_SIZE

NEG_LARGE = -1e30
LOG2_SCALE = math.log2(math.e) / math.sqrt(HEAD_SIZE)

SIDE = 4
LOCAL_HEADS = KEY_VALUE_HEADS // 2
PAIR = LOCAL_HEADS // 2
PAIR_WIDTH = PAIR * HEAD_SIZE
MESH = pl.DeviceIdType.MESH

NEAR, FAR, RESULT, SHARE, COPIES = 3, 11, 43, 45, 48

SHARED = 6
KEPT = PAIR * GROUP - SHARED


def dot_nt(a, b):
    return lax.dot_general(a, b, (((1,), (1,)), ((), ())), preferred_element_type=jnp.float32)


def wrap(x):
    return lax.rem(x + SIDE, SIDE)


def order_of(index, half, core):
    return jnp.where(index < half, core * half + index, (1 - core) * half + index - half)


def kernel(
    q_hbm, kv_hbm, short_q_hbm, short_kv_hbm, seg, out_hbm, short_out_hbm,
    q, kv, acc, high, total, result, q_extra, result_extra, short_q, short_kv, send, recv, local,
):
    half = q_hbm.shape[0]
    rows = 2 * half
    ctx, head = lax.axis_index("ctx"), lax.axis_index("head")
    y, z, core = lax.div(ctx, 2), lax.rem(ctx, 2) * 2 + lax.div(head, 2), lax.rem(head, 2)
    chip = y * SIDE + z
    q_columns = LOCAL_HEADS * WIDE

    def device(to_y, to_z, to_core):
        return {"ctx": to_y * 2 + lax.div(to_z, 2), "head": lax.rem(to_z, 2) * 2 + to_core}

    mate = device(y, z, 1 - core)
    ahead = (device(y, wrap(z + 1), core), device(wrap(y + 1), z, core))
    behind = (device(y, wrap(z - 1), core), device(wrap(y - 1), z, core))

    def remote(src, dst, index, target):
        return pltpu.make_async_remote_copy(
            src_ref=src, dst_ref=dst, send_sem=send.at[index], recv_sem=recv.at[index], device_id=target, device_id_type=MESH
        )

    def mine_columns(side, of_core):
        start = of_core * (LOCAL_HEADS * HEAD_SIZE) + side * PAIR_WIDTH
        return pl.ds(pl.multiple_of(start, PAIR_WIDTH), PAIR_WIDTH)

    def heads_of(of_core, start, size):
        return pl.ds(pl.multiple_of(of_core * q_columns + start, 2 * HEAD_SIZE), size)

    def mate_kv(side):
        return remote(kv_hbm.at[:, :, mine_columns(side, 1 - core)], kv.at[side, 0, :, 0, pl.ds(half, half)], 1 + side, mate)

    def mate_q():
        return remote(q_hbm.at[:, heads_of(1 - core, 0, q_columns)], q.at[1], 0, mate)

    def near(side, which):
        index = NEAR + 4 * side + which
        if which == 0:
            return remote(kv.at[side, 0, :, 0], kv.at[side, 0, :, 1], index, ahead[side])
        if which == 1:
            return remote(kv.at[side, 0, :, 0], kv.at[side, 0, :, 2], index, behind[side])
        if which == 2:
            return remote(kv.at[side, 0, 0, 1], kv.at[side, 0, 0, 3], index, ahead[side])
        return remote(kv.at[side, 0, 1, 2], kv.at[side, 0, 1, 3], index, behind[side])

    def from_behind(side, piece, at_y):
        both = jnp.logical_or(side == 1, at_y == SIDE - 1)
        return jnp.where(both, 1 + piece // 2, 1), jnp.where(both, 2 * (piece % 2), piece)

    def from_ahead(side, piece, at_y):
        both = jnp.logical_or(side == 1, at_y == SIDE - 1)
        return jnp.where(both, 1 + piece // 2, 2), jnp.where(both, 2 * (piece % 2) + 1, piece)

    def far(side, piece, which):
        index = FAR + 16 * side + 4 * piece + which
        if which == 0:
            unit, slot = from_behind(side, piece, wrap(y + 1))
            return remote(kv.at[side, 0, :, piece], kv.at[side, unit, :, slot], index, ahead[1 - side])
        if which == 1:
            unit, slot = from_ahead(side, piece, wrap(y - 1))
            return remote(kv.at[side, 0, :, piece], kv.at[side, unit, :, slot], index, behind[1 - side])
        if which == 2:
            unit, slot = from_behind(side, piece, y)
            return remote(kv.at[side, unit, 0, slot], kv.at[side, 3, 0, piece], index, ahead[1 - side])
        unit, slot = from_ahead(side, piece, y)
        return remote(kv.at[side, unit, 1, slot], kv.at[side, 3, 1, piece], index, behind[1 - side])

    def give_back(side, width):
        columns = heads_of(core, side * (PAIR * WIDE), width)
        return remote(result.at[1, side, :, pl.ds(0, width)], out_hbm.at[:, columns], RESULT + side, mate)

    def keep(side, width):
        columns = heads_of(core, side * (PAIR * WIDE), width)
        return pltpu.make_async_copy(result.at[0, side, :, pl.ds(0, width)], out_hbm.at[:, columns], local.at[5 + side])

    gives, takes = y >= SIDE // 2, y < SIDE // 2
    partner, crossed = device(SIDE - 1 - y, z, core), device(SIDE - 1 - y, z, 1 - core)
    whole, part_width = PAIR * WIDE, KEPT * HEAD_SIZE

    def share_q():
        return remote(q.at[:, :, pl.ds(part_width, SHARED * HEAD_SIZE)], q_extra, SHARE, partner)

    def share_result(who):
        columns = heads_of(core, part_width, SHARED * HEAD_SIZE)
        target = partner if who == 0 else crossed
        return remote(result_extra.at[who], out_hbm.at[:, columns], SHARE + 1 + who, target)

    own_q = pltpu.make_async_copy(q_hbm.at[:, heads_of(core, 0, q_columns)], q.at[0], local.at[0])
    own_kv = [
        pltpu.make_async_copy(kv_hbm.at[:, :, mine_columns(side, core)], kv.at[side, 0, :, 0, pl.ds(0, half)], local.at[1 + side])
        for side in range(2)
    ]
    get_short_q = pltpu.make_async_copy(short_q_hbm, short_q, local.at[3])
    get_short_kv = pltpu.make_async_copy(short_kv_hbm, short_kv, local.at[4])
    put_short = pltpu.make_async_copy(short_q, short_out_hbm, local.at[7])

    own_kv[0].start()
    own_kv[1].start()
    get_short_kv.start()
    get_short_q.start()
    own_q.start()
    barrier = pltpu.get_barrier_semaphore()
    for target in (mate, crossed) + ahead + behind:
        pl.semaphore_signal(barrier, inc=1, device_id=target, device_id_type=MESH)
    pl.semaphore_wait(barrier, 6)
    for side in range(2):
        mate_kv(side).start()
    mate_q().start()
    for side in range(2):
        own_kv[side].wait()
        mate_kv(side).wait_recv()
        near(side, 0).start()
        near(side, 1).start()
    tokens = short_q.shape[0]
    part_rows = tokens // 2
    seg_row = seg[...].astype(jnp.float32)
    seg_col = jnp.broadcast_to(seg_row, (HEAD_SIZE, tokens)).T

    def short_head(g, carry):
        key_columns = pl.ds(pl.multiple_of(g * HEAD_SIZE, HEAD_SIZE), HEAD_SIZE)
        k, v = short_kv[0, :, key_columns], short_kv[1, :, key_columns]
        v_one = jnp.concatenate([v, jnp.ones_like(v)], axis=1)
        columns = [pl.ds(pl.multiple_of(g * WIDE + h * HEAD_SIZE, HEAD_SIZE), HEAD_SIZE) for h in range(GROUP)]
        for part in range(2):
            low, keys = part * part_rows, (part + 1) * part_rows
            q_pos = low + lax.broadcasted_iota(jnp.int32, (part_rows, keys), 0)
            k_pos = lax.broadcasted_iota(jnp.int32, (part_rows, keys), 1)
            same = seg_col[low : low + part_rows, :1] == seg_row[:1, :keys]
            allowed = (k_pos <= q_pos) & same
            weights = []
            for s in [dot_nt(short_q[low : low + part_rows, c], k[:keys]) for c in columns]:
                s = jnp.where(allowed, s, NEG_LARGE)
                top = jnp.max(s, axis=1, keepdims=True)
                weights.append(jnp.exp2((s - top) * LOG2_SCALE).astype(jnp.bfloat16))
            mixes = [jnp.dot(p, v_one[:keys], preferred_element_type=jnp.float32) for p in weights]
            for c, mixed in zip(columns, mixes):
                short_q[low : low + part_rows, c] = (mixed[:, :HEAD_SIZE] / mixed[:, HEAD_SIZE:]).astype(jnp.bfloat16)
        return carry

    get_short_kv.wait()
    get_short_q.wait()

    def short_step(g, carry):
        short_head(g, carry)

        @pl.when(g == 5)
        def _():
            for side in range(2):
                near(side, 0).wait_recv()
                near(side, 2).start()
                near(side, 1).wait_recv()
                near(side, 3).start()
            for piece in (0, 1, 2):
                for side in range(2):
                    far(side, piece, 0).start()
                    far(side, piece, 1).start()

        return carry

    lax.fori_loop(0, KEY_VALUE_HEADS, short_step, 0)
    put_short.start()
    own_q.wait()
    mate_q().wait_recv()

    for side in range(2):
        near(side, 2).wait_recv()
        near(side, 3).wait_recv()
        far(side, 3, 0).start()
        far(side, 3, 1).start()

    @pl.when(gives)
    def _():
        share_q().start()

    q_pos = chip * rows + order_of(lax.broadcasted_iota(jnp.int32, (rows, 1), 0), half, core)
    key_index = order_of(lax.broadcasted_iota(jnp.int32, (1, rows), 1), half, core)

    def owners_of(unit, side):
        owners = []
        for slot in range(SIDE):
            both = jnp.logical_or(side == 1, y == SIDE - 1)
            beyond = jnp.where(both, slot // 2 + 2 * (unit - 1), slot)
            ring = jnp.where(jnp.logical_or(unit == 0, unit == 3), slot, beyond)
            next_to = jnp.where(both, 2 * (slot % 2) - 1, 2 * unit - 3)
            along = jnp.where(ring == 1, -1, jnp.where(ring == 2, 1, jnp.where(ring == 3, 2, 0)))
            across = jnp.where(unit == 0, 0, jnp.where(unit == 3, 2, next_to))
            owner_y = wrap(y + jnp.where(side == 0, across, along))
            owner_z = wrap(z + jnp.where(side == 0, along, across))
            owners.append(owner_y * SIDE + owner_z)
        return owners

    def phase(number, carry):
        unit = lax.div(number, 2)
        side = jnp.where(unit == 1, 1 - lax.rem(number, 2), lax.rem(number, 2))
        owners = owners_of(unit, side)
        low = jnp.minimum(jnp.minimum(owners[0], owners[1]), jnp.minimum(owners[2], owners[3]))
        top = jnp.maximum(jnp.maximum(owners[0], owners[1]), jnp.maximum(owners[2], owners[3]))

        def block(local_head, plane, of_side=side, of_unit=unit):
            columns = pl.ds(pl.multiple_of(local_head * HEAD_SIZE, HEAD_SIZE), HEAD_SIZE)
            return kv[of_side, of_unit, plane, :, :, columns].reshape(SIDE * rows, HEAD_SIZE)

        def scores(item, k):
            columns = pl.ds(pl.multiple_of((side * PAIR * GROUP + item) * HEAD_SIZE, HEAD_SIZE), HEAD_SIZE)
            query = jnp.concatenate([q[0, :, columns], q[1, :, columns]], axis=0)
            return dot_nt(query, k)

        def update(place, s, v, owners, positions, first):
            v_one = jnp.concatenate([v, jnp.ones_like(v)], axis=1)
            if owners is not None:
                k_pos = jnp.concatenate([owner * rows + key_index for owner in owners], axis=1)
                s = jnp.where(k_pos <= positions, s, NEG_LARGE)
            r = pl.ds(pl.multiple_of(place * rows, rows), rows)
            best = jnp.max(s, axis=1, keepdims=True) * LOG2_SCALE
            if first:
                new = jnp.broadcast_to(best, (rows, HEAD_SIZE))
            else:
                old = high[r, :]
                new = jnp.maximum(old, best)
                factor = jnp.exp2(old - new)
            p = jnp.exp2(s * LOG2_SCALE - new[:, :1]).astype(jnp.bfloat16)
            mixed = jnp.dot(p, v_one, preferred_element_type=jnp.float32)
            high[r, :] = new
            if first:
                acc[r, :] = mixed[:, :HEAD_SIZE]
                total[r, :] = mixed[:, HEAD_SIZE:]
            else:
                acc[r, :] = acc[r, :] * factor + mixed[:, :HEAD_SIZE]
                total[r, :] = total[r, :] * factor + mixed[:, HEAD_SIZE:]

        def run(masked, first, begin=0, straight=PAIR * GROUP):
            def some_heads(turn, inner):
                count = GROUP if masked else straight
                start = turn * GROUP + begin
                s = scores(start, block(turn + begin // GROUP, 0))
                for h in range(count):
                    local_head = turn + (begin + h) // GROUP
                    following = turn + (begin + h + 1) // GROUP
                    ahead_s = scores(start + h + 1, block(following, 0)) if h + 1 < count else None
                    place = side * PAIR * GROUP + start + h
                    update(place, s, block(local_head, 1), owners if masked else None, q_pos, first)
                    s = ahead_s
                return inner

            if masked:
                lax.fori_loop(0, PAIR, some_heads, 0)
            else:
                some_heads(0, 0)

        @pl.when(unit == 0)
        def _():
            run(True, True)

        used = jnp.logical_and(unit > 0, low <= chip)

        clear = jnp.logical_and(used, top < chip)
        fewer = jnp.logical_and(gives, side == 0)

        @pl.when(clear)
        def _():
            run(False, False, 0, KEPT)

        @pl.when(jnp.logical_and(clear, jnp.logical_not(fewer)))
        def _():
            run(False, False, KEPT, SHARED)

        @pl.when(jnp.logical_and(used, top >= chip))
        def _():
            run(True, False)

        def pass_on(pieces):
            for piece in pieces:
                for side in range(2):
                    far(side, piece, 0).wait_recv()
                    far(side, piece, 2).start()
                    far(side, piece, 1).wait_recv()
                    far(side, piece, 3).start()

        @pl.when(number == 0)
        def _():
            pass_on((0,))

        @pl.when(number == 1)
        def _():
            pass_on((1,))

        @pl.when(number == jnp.where(y == SIDE - 1, 3, 2))
        def _():
            pass_on((2, 3))

        @pl.when(number == 5)
        def _():
            for piece in range(SIDE):
                for side in range(2):
                    far(side, piece, 2).wait_recv()
                    far(side, piece, 3).wait_recv()

        extra = LOCAL_HEADS * GROUP

        @pl.when(jnp.logical_and(takes, number == 3))
        def _():
            share_q().wait_recv()
            area = pl.ds(extra * rows, SHARED * rows)
            acc[area, :] = jnp.zeros((SHARED * rows, HEAD_SIZE), jnp.float32)
            total[area, :] = jnp.zeros((SHARED * rows, HEAD_SIZE), jnp.float32)
            high[area, :] = jnp.full((SHARED * rows, HEAD_SIZE), NEG_LARGE, jnp.float32)

        @pl.when(jnp.logical_and(takes, jnp.logical_or(number == 3, number == 5)))
        def _():
            def shared_unit(of_unit, inner):
                local_head = KEPT // GROUP
                k, v = block(local_head, 0, 0, of_unit), block(local_head, 1, 0, of_unit)
                positions = q_pos + (SIDE - 1 - 2 * y) * SIDE * rows
                of_row = owners_of(of_unit, 0)

                def shared_scores(h):
                    columns = slice(h * HEAD_SIZE, (h + 1) * HEAD_SIZE)
                    return dot_nt(jnp.concatenate([q_extra[0, :, columns], q_extra[1, :, columns]], axis=0), k)

                s = shared_scores(0)
                for h in range(SHARED):
                    ahead_s = shared_scores(h + 1) if h + 1 < SHARED else None
                    update(extra + h, s, v, of_row, positions, False)
                    s = ahead_s
                return inner

            lax.fori_loop(jnp.where(number == 3, 0, 3), jnp.where(number == 3, 3, jnp.where(y == 0, 4, 3)), shared_unit, 0)

        @pl.when(jnp.logical_and(takes, number == 5))
        def _():
            for h in range(SHARED):
                for who in range(2):
                    part = pl.ds((extra + h) * rows + who * half, half)
                    result_extra[who, :, h * HEAD_SIZE : (h + 1) * HEAD_SIZE] = (acc[part, :] / total[part, :]).astype(jnp.bfloat16)
            share_result(0).start()
            share_result(1).start()

        @pl.when(unit == 3)
        def _():
            def divide(item, inner):
                r = pl.multiple_of((side * PAIR * GROUP + item) * rows, rows)
                columns = pl.ds(pl.multiple_of(item * HEAD_SIZE, HEAD_SIZE), HEAD_SIZE)
                for who in range(2):
                    part = pl.ds(r + who * half, half)
                    result[who, side, :, columns] = (acc[part, :] / total[part, :]).astype(jnp.bfloat16)
                return inner

            lax.fori_loop(0, PAIR * GROUP, divide, 0)

        @pl.when(jnp.logical_and(number == 6, gives))
        def _():
            give_back(0, part_width).start()
            keep(0, part_width).start()

        @pl.when(jnp.logical_and(number == 6, jnp.logical_not(gives)))
        def _():
            give_back(0, whole).start()
            keep(0, whole).start()

        @pl.when(number == 7)
        def _():
            give_back(1, whole).start()
            keep(1, whole).start()

        return carry

    lax.fori_loop(0, 8, phase, 0)

    put_short.wait()
    def finish(side, width):
        keep(side, width).wait()
        give_back(side, width).wait_recv()
        give_back(side, width).wait_send()

    finish(1, whole)

    @pl.when(gives)
    def _():
        finish(0, part_width)
        share_q().wait_send()
        share_result(0).wait_recv()
        share_result(1).wait_recv()

    @pl.when(jnp.logical_not(gives))
    def _():
        finish(0, whole)

    @pl.when(takes)
    def _():
        share_result(0).wait_send()
        share_result(1).wait_send()

    for side in range(2):
        mate_kv(side).wait_send()
        for which in range(4):
            near(side, which).wait_send()
            for piece in range(SIDE):
                far(side, piece, which).wait_send()
    mate_q().wait_send()


def on_device(long_query, long_kv, short_query, short_key_value, short_seg):
    half = long_query.shape[0]
    rows = 2 * half
    state_rows = (LOCAL_HEADS * GROUP + SHARED) * rows
    anywhere = pl.BlockSpec(memory_space=pl.ANY)
    vmem = pl.BlockSpec(memory_space=pltpu.VMEM)
    return pl.pallas_call(
        kernel,
        out_shape=(
            jax.ShapeDtypeStruct(long_query.shape, long_query.dtype),
            jax.ShapeDtypeStruct(short_query.shape, short_query.dtype),
        ),
        in_specs=[anywhere] * 4 + [vmem],
        out_specs=(anywhere, anywhere),
        scratch_shapes=[
            pltpu.VMEM((2, half, LOCAL_HEADS * WIDE), jnp.bfloat16),
            pltpu.VMEM((2, 4, 2, SIDE, rows, PAIR_WIDTH), jnp.bfloat16),
            pltpu.VMEM((state_rows, HEAD_SIZE), jnp.float32),
            pltpu.VMEM((state_rows, HEAD_SIZE), jnp.float32),
            pltpu.VMEM((state_rows, HEAD_SIZE), jnp.float32),
            pltpu.VMEM((2, 2, half, PAIR * WIDE), jnp.bfloat16),
            pltpu.VMEM((2, half, SHARED * HEAD_SIZE), jnp.bfloat16),
            pltpu.VMEM((2, half, SHARED * HEAD_SIZE), jnp.bfloat16),
            pltpu.VMEM(short_query.shape, jnp.bfloat16),
            pltpu.VMEM(short_key_value.shape, jnp.bfloat16),
            pltpu.SemaphoreType.DMA((COPIES,)),
            pltpu.SemaphoreType.DMA((COPIES,)),
            pltpu.SemaphoreType.DMA((8,)),
        ],
        compiler_params=pltpu.CompilerParams(
            collective_id=0, has_side_effects=True, vmem_limit_bytes=63 << 20
        ),
        name="window_attention",
    )(long_query, long_kv, short_query, short_key_value, short_seg)


def solution(mesh):
    return jax.shard_map(
        on_device,
        mesh=mesh,
        in_specs=(
            P(("dp", "ctx", "head"), None),
            P(None, ("dp", "ctx", "head"), None),
            P(("dp", "ctx", "head"), None),
            P(None, ("dp", "ctx", "head"), None),
            P(("dp", "ctx", "head"), None),
        ),
        out_specs=(P(("dp", "ctx", "head"), None), P(("dp", "ctx", "head"), None)),
        check_vma=False,
    )
```

```python
import functools
import math

import jax
import jax.numpy as jnp
from jax import lax
from jax.experimental import pallas as pl
from jax.experimental.pallas import tpu as pltpu
from jax.sharding import PartitionSpec as P

QUERY_HEAD_COUNT = 64
KEY_VALUE_HEADS = 8
HEAD_SIZE = 128
GROUP = QUERY_HEAD_COUNT // KEY_VALUE_HEADS
WIDE = GROUP * HEAD_SIZE

NEG_LARGE = -1e30
LOG2_SCALE = math.log2(math.e) / math.sqrt(HEAD_SIZE)

SIDE = 4
LOCAL_HEADS = KEY_VALUE_HEADS // 2
PAIR = LOCAL_HEADS // 2
PAIR_WIDTH = PAIR * HEAD_SIZE
MESH = pl.DeviceIdType.MESH

NEAR, FAR, RESULT, SHARE, SECOND, COPIES = 3, 11, 43, 45, 48, 52

SHARED = 6
KEPT = PAIR * GROUP - SHARED


def dot_nt(a, b):
    return lax.dot_general(a, b, (((1,), (1,)), ((), ())), preferred_element_type=jnp.float32)


def wrap(x):
    return lax.rem(x + SIDE, SIDE)


def order_of(index, half, core):
    return jnp.where(index < half, core * half + index, (1 - core) * half + index - half)


def kernel(
    q_hbm, kv_hbm, short_q_hbm, short_kv_hbm, seg, out_hbm, short_out_hbm,
    q, kv, acc, high, total, result, q_extra, result_extra, short_q, short_kv, send, recv, local,
):
    half = q_hbm.shape[0]
    rows = 2 * half
    ctx, head = lax.axis_index("ctx"), lax.axis_index("head")
    y, z, core = lax.div(ctx, 2), lax.rem(ctx, 2) * 2 + lax.div(head, 2), lax.rem(head, 2)
    chip = y * SIDE + z
    q_columns = LOCAL_HEADS * WIDE

    def device(to_y, to_z, to_core):
        return {"ctx": to_y * 2 + lax.div(to_z, 2), "head": lax.rem(to_z, 2) * 2 + to_core}

    mate = device(y, z, 1 - core)
    ahead = (device(y, wrap(z + 1), core), device(wrap(y + 1), z, core))
    behind = (device(y, wrap(z - 1), core), device(wrap(y - 1), z, core))

    def remote(src, dst, index, target):
        return pltpu.make_async_remote_copy(
            src_ref=src, dst_ref=dst, send_sem=send.at[index], recv_sem=recv.at[index], device_id=target, device_id_type=MESH
        )

    def mine_columns(side, of_core):
        start = of_core * (LOCAL_HEADS * HEAD_SIZE) + side * PAIR_WIDTH
        return pl.ds(pl.multiple_of(start, PAIR_WIDTH), PAIR_WIDTH)

    def heads_of(of_core, start, size):
        return pl.ds(pl.multiple_of(of_core * q_columns + start, 2 * HEAD_SIZE), size)

    def mate_kv(side):
        return remote(kv_hbm.at[:, :, mine_columns(side, 1 - core)], kv.at[side, 0, :, 0, pl.ds(half, half)], 1 + side, mate)

    def mate_q():
        return remote(q_hbm.at[:, heads_of(1 - core, 0, q_columns)], q.at[1], 0, mate)

    def first_hop(side, which, part):
        index = NEAR + 4 * side + which if part == 0 else SECOND + 2 * side + which
        tokens = pl.ds(part * half, half)
        target = ahead[side] if which == 0 else behind[side]
        return remote(kv.at[side, 0, :, 0, tokens], kv.at[side, 0, :, 1 + which, tokens], index, target)

    def near(side, which):
        index = NEAR + 4 * side + which
        if which == 2:
            return remote(kv.at[side, 0, 0, 1], kv.at[side, 0, 0, 3], index, ahead[side])
        return remote(kv.at[side, 0, 1, 2], kv.at[side, 0, 1, 3], index, behind[side])

    def from_behind(side, piece, at_y):
        both = jnp.logical_or(side == 1, at_y == SIDE - 1)
        return jnp.where(both, 1 + piece // 2, 1), jnp.where(both, 2 * (piece % 2), piece)

    def from_ahead(side, piece, at_y):
        both = jnp.logical_or(side == 1, at_y == SIDE - 1)
        return jnp.where(both, 1 + piece // 2, 2), jnp.where(both, 2 * (piece % 2) + 1, piece)

    def far(side, piece, which):
        index = FAR + 16 * side + 4 * piece + which
        if which == 0:
            unit, slot = from_behind(side, piece, wrap(y + 1))
            return remote(kv.at[side, 0, :, piece], kv.at[side, unit, :, slot], index, ahead[1 - side])
        if which == 1:
            unit, slot = from_ahead(side, piece, wrap(y - 1))
            return remote(kv.at[side, 0, :, piece], kv.at[side, unit, :, slot], index, behind[1 - side])
        if which == 2:
            unit, slot = from_behind(side, piece, y)
            return remote(kv.at[side, unit, 0, slot], kv.at[side, 3, 0, piece], index, ahead[1 - side])
        unit, slot = from_ahead(side, piece, y)
        return remote(kv.at[side, unit, 1, slot], kv.at[side, 3, 1, piece], index, behind[1 - side])

    def give_back(side, width):
        columns = heads_of(core, side * (PAIR * WIDE), width)
        return remote(result.at[1, side, :, pl.ds(0, width)], out_hbm.at[:, columns], RESULT + side, mate)

    def keep(side, width):
        columns = heads_of(core, side * (PAIR * WIDE), width)
        return pltpu.make_async_copy(result.at[0, side, :, pl.ds(0, width)], out_hbm.at[:, columns], local.at[5 + side])

    gives, takes = y >= SIDE // 2, y < SIDE // 2
    partner, crossed = device(SIDE - 1 - y, z, core), device(SIDE - 1 - y, z, 1 - core)
    whole, part_width = PAIR * WIDE, KEPT * HEAD_SIZE

    def share_q():
        return remote(q.at[:, :, pl.ds(part_width, SHARED * HEAD_SIZE)], q_extra, SHARE, partner)

    def share_result(who):
        columns = heads_of(core, part_width, SHARED * HEAD_SIZE)
        target = partner if who == 0 else crossed
        return remote(result_extra.at[who], out_hbm.at[:, columns], SHARE + 1 + who, target)

    own_q = pltpu.make_async_copy(q_hbm.at[:, heads_of(core, 0, q_columns)], q.at[0], local.at[0])
    own_kv = [
        pltpu.make_async_copy(kv_hbm.at[:, :, mine_columns(side, core)], kv.at[side, 0, :, 0, pl.ds(0, half)], local.at[1 + side])
        for side in range(2)
    ]
    get_short_q = pltpu.make_async_copy(short_q_hbm, short_q, local.at[3])
    get_short_kv = pltpu.make_async_copy(short_kv_hbm, short_kv, local.at[4])
    put_short = pltpu.make_async_copy(short_q, short_out_hbm, local.at[7])

    own_kv[0].start()
    own_kv[1].start()
    get_short_kv.start()
    get_short_q.start()
    own_q.start()
    barrier = pltpu.get_barrier_semaphore()
    for target in (mate, crossed) + ahead + behind:
        pl.semaphore_signal(barrier, inc=1, device_id=target, device_id_type=MESH)
    pl.semaphore_wait(barrier, 6)
    for side in range(2):
        mate_kv(side).start()
    mate_q().start()
    for side in range(2):
        own_kv[side].wait()
        first_hop(side, 0, 0).start()
        first_hop(side, 1, 0).start()
    for side in range(2):
        mate_kv(side).wait_recv()
        first_hop(side, 0, 1).start()
        first_hop(side, 1, 1).start()
    tokens = short_q.shape[0]
    part_rows = tokens // 2
    seg_row = seg[...].astype(jnp.float32)
    seg_col = jnp.broadcast_to(seg_row, (HEAD_SIZE, tokens)).T

    def short_head(g, carry):
        key_columns = pl.ds(pl.multiple_of(g * HEAD_SIZE, HEAD_SIZE), HEAD_SIZE)
        k, v = short_kv[0, :, key_columns], short_kv[1, :, key_columns]
        v_one = jnp.concatenate([v, jnp.ones_like(v)], axis=1)
        columns = [pl.ds(pl.multiple_of(g * WIDE + h * HEAD_SIZE, HEAD_SIZE), HEAD_SIZE) for h in range(GROUP)]
        for part in range(2):
            low, keys = part * part_rows, (part + 1) * part_rows
            q_pos = low + lax.broadcasted_iota(jnp.int32, (part_rows, keys), 0)
            k_pos = lax.broadcasted_iota(jnp.int32, (part_rows, keys), 1)
            same = seg_col[low : low + part_rows, :1] == seg_row[:1, :keys]
            allowed = (k_pos <= q_pos) & same
            weights = []
            for s in [dot_nt(short_q[low : low + part_rows, c], k[:keys]) for c in columns]:
                s = jnp.where(allowed, s, NEG_LARGE)
                top = jnp.max(s, axis=1, keepdims=True)
                weights.append(jnp.exp2((s - top) * LOG2_SCALE).astype(jnp.bfloat16))
            mixes = [jnp.dot(p, v_one[:keys], preferred_element_type=jnp.float32) for p in weights]
            for c, mixed in zip(columns, mixes):
                short_q[low : low + part_rows, c] = (mixed[:, :HEAD_SIZE] / mixed[:, HEAD_SIZE:]).astype(jnp.bfloat16)
        return carry

    get_short_kv.wait()
    get_short_q.wait()

    def short_step(g, carry):
        short_head(g, carry)

        @pl.when(g == 5)
        def _():
            for side in range(2):
                first_hop(side, 0, 0).wait_recv()
                first_hop(side, 0, 1).wait_recv()
                near(side, 2).start()
                first_hop(side, 1, 0).wait_recv()
                first_hop(side, 1, 1).wait_recv()
                near(side, 3).start()
            for piece in (0, 1, 2):
                for side in range(2):
                    far(side, piece, 0).start()
                    far(side, piece, 1).start()

        return carry

    lax.fori_loop(0, KEY_VALUE_HEADS, short_step, 0)
    put_short.start()
    own_q.wait()
    mate_q().wait_recv()

    for side in range(2):
        near(side, 2).wait_recv()
        near(side, 3).wait_recv()
        far(side, 3, 0).start()
        far(side, 3, 1).start()

    @pl.when(gives)
    def _():
        share_q().start()

    q_pos = chip * rows + order_of(lax.broadcasted_iota(jnp.int32, (rows, 1), 0), half, core)
    key_index = order_of(lax.broadcasted_iota(jnp.int32, (1, rows), 1), half, core)

    def owners_of(unit, side):
        owners = []
        for slot in range(SIDE):
            both = jnp.logical_or(side == 1, y == SIDE - 1)
            beyond = jnp.where(both, slot // 2 + 2 * (unit - 1), slot)
            ring = jnp.where(jnp.logical_or(unit == 0, unit == 3), slot, beyond)
            next_to = jnp.where(both, 2 * (slot % 2) - 1, 2 * unit - 3)
            along = jnp.where(ring == 1, -1, jnp.where(ring == 2, 1, jnp.where(ring == 3, 2, 0)))
            across = jnp.where(unit == 0, 0, jnp.where(unit == 3, 2, next_to))
            owner_y = wrap(y + jnp.where(side == 0, across, along))
            owner_z = wrap(z + jnp.where(side == 0, along, across))
            owners.append(owner_y * SIDE + owner_z)
        return owners

    def phase(number, carry):
        unit = lax.div(number, 2)
        side = jnp.where(unit == 1, 1 - lax.rem(number, 2), lax.rem(number, 2))
        owners = owners_of(unit, side)
        low = jnp.minimum(jnp.minimum(owners[0], owners[1]), jnp.minimum(owners[2], owners[3]))
        top = jnp.maximum(jnp.maximum(owners[0], owners[1]), jnp.maximum(owners[2], owners[3]))

        def block(local_head, plane, of_side=side, of_unit=unit):
            columns = pl.ds(pl.multiple_of(local_head * HEAD_SIZE, HEAD_SIZE), HEAD_SIZE)
            return kv[of_side, of_unit, plane, :, :, columns].reshape(SIDE * rows, HEAD_SIZE)

        def scores(item, k):
            columns = pl.ds(pl.multiple_of((side * PAIR * GROUP + item) * HEAD_SIZE, HEAD_SIZE), HEAD_SIZE)
            query = jnp.concatenate([q[0, :, columns], q[1, :, columns]], axis=0)
            return dot_nt(query, k)

        def update(place, s, v, owners, positions, first):
            v_one = jnp.concatenate([v, jnp.ones_like(v)], axis=1)
            if owners is not None:
                k_pos = jnp.concatenate([owner * rows + key_index for owner in owners], axis=1)
                s = jnp.where(k_pos <= positions, s, NEG_LARGE)
            r = pl.ds(pl.multiple_of(place * rows, rows), rows)
            best = jnp.max(s, axis=1, keepdims=True) * LOG2_SCALE
            if first:
                new = jnp.broadcast_to(best, (rows, HEAD_SIZE))
            else:
                old = high[r, :]
                new = jnp.maximum(old, best)
                factor = jnp.exp2(old - new)
            p = jnp.exp2(s * LOG2_SCALE - new[:, :1]).astype(jnp.bfloat16)
            mixed = jnp.dot(p, v_one, preferred_element_type=jnp.float32)
            high[r, :] = new
            if first:
                acc[r, :] = mixed[:, :HEAD_SIZE]
                total[r, :] = mixed[:, HEAD_SIZE:]
            else:
                acc[r, :] = acc[r, :] * factor + mixed[:, :HEAD_SIZE]
                total[r, :] = total[r, :] * factor + mixed[:, HEAD_SIZE:]

        def run(masked, first, begin=0, straight=PAIR * GROUP):
            def some_heads(turn, inner):
                count = GROUP if masked else straight
                start = turn * GROUP + begin
                s = scores(start, block(turn + begin // GROUP, 0))
                for h in range(count):
                    local_head = turn + (begin + h) // GROUP
                    following = turn + (begin + h + 1) // GROUP
                    ahead_s = scores(start + h + 1, block(following, 0)) if h + 1 < count else None
                    place = side * PAIR * GROUP + start + h
                    update(place, s, block(local_head, 1), owners if masked else None, q_pos, first)
                    s = ahead_s
                return inner

            if masked:
                lax.fori_loop(0, PAIR, some_heads, 0)
            else:
                some_heads(0, 0)

        @pl.when(unit == 0)
        def _():
            run(True, True)

        used = jnp.logical_and(unit > 0, low <= chip)

        clear = jnp.logical_and(used, top < chip)
        fewer = jnp.logical_and(gives, side == 0)

        @pl.when(clear)
        def _():
            run(False, False, 0, KEPT)

        @pl.when(jnp.logical_and(clear, jnp.logical_not(fewer)))
        def _():
            run(False, False, KEPT, SHARED)

        @pl.when(jnp.logical_and(used, top >= chip))
        def _():
            run(True, False)

        def pass_on(pieces):
            for piece in pieces:
                for side in range(2):
                    far(side, piece, 0).wait_recv()
                    far(side, piece, 2).start()
                    far(side, piece, 1).wait_recv()
                    far(side, piece, 3).start()

        @pl.when(number == 0)
        def _():
            pass_on((0,))

        @pl.when(number == 1)
        def _():
            pass_on((1,))

        @pl.when(number == jnp.where(y == SIDE - 1, 3, 2))
        def _():
            pass_on((2, 3))

        @pl.when(number == 5)
        def _():
            for piece in range(SIDE):
                for side in range(2):
                    far(side, piece, 2).wait_recv()
                    far(side, piece, 3).wait_recv()

        extra = LOCAL_HEADS * GROUP

        @pl.when(jnp.logical_and(takes, number == 3))
        def _():
            share_q().wait_recv()
            area = pl.ds(extra * rows, SHARED * rows)
            acc[area, :] = jnp.zeros((SHARED * rows, HEAD_SIZE), jnp.float32)
            total[area, :] = jnp.zeros((SHARED * rows, HEAD_SIZE), jnp.float32)
            high[area, :] = jnp.full((SHARED * rows, HEAD_SIZE), NEG_LARGE, jnp.float32)

        @pl.when(jnp.logical_and(takes, jnp.logical_or(number == 3, number == 5)))
        def _():
            def shared_unit(of_unit, inner):
                local_head = KEPT // GROUP
                k, v = block(local_head, 0, 0, of_unit), block(local_head, 1, 0, of_unit)
                positions = q_pos + (SIDE - 1 - 2 * y) * SIDE * rows
                of_row = owners_of(of_unit, 0)

                def shared_scores(h):
                    columns = slice(h * HEAD_SIZE, (h + 1) * HEAD_SIZE)
                    return dot_nt(jnp.concatenate([q_extra[0, :, columns], q_extra[1, :, columns]], axis=0), k)

                s = shared_scores(0)
                for h in range(SHARED):
                    ahead_s = shared_scores(h + 1) if h + 1 < SHARED else None
                    update(extra + h, s, v, of_row, positions, False)
                    s = ahead_s
                return inner

            lax.fori_loop(jnp.where(number == 3, 0, 3), jnp.where(number == 3, 3, jnp.where(y == 0, 4, 3)), shared_unit, 0)

        @pl.when(jnp.logical_and(takes, number == 5))
        def _():
            for h in range(SHARED):
                for who in range(2):
                    part = pl.ds((extra + h) * rows + who * half, half)
                    result_extra[who, :, h * HEAD_SIZE : (h + 1) * HEAD_SIZE] = (acc[part, :] / total[part, :]).astype(jnp.bfloat16)
            share_result(0).start()
            share_result(1).start()

        @pl.when(unit == 3)
        def _():
            def divide(item, inner):
                r = pl.multiple_of((side * PAIR * GROUP + item) * rows, rows)
                columns = pl.ds(pl.multiple_of(item * HEAD_SIZE, HEAD_SIZE), HEAD_SIZE)
                for who in range(2):
                    part = pl.ds(r + who * half, half)
                    result[who, side, :, columns] = (acc[part, :] / total[part, :]).astype(jnp.bfloat16)
                return inner

            lax.fori_loop(0, PAIR * GROUP, divide, 0)

        @pl.when(jnp.logical_and(number == 6, gives))
        def _():
            give_back(0, part_width).start()
            keep(0, part_width).start()

        @pl.when(jnp.logical_and(number == 6, jnp.logical_not(gives)))
        def _():
            give_back(0, whole).start()
            keep(0, whole).start()

        @pl.when(number == 7)
        def _():
            give_back(1, whole).start()
            keep(1, whole).start()

        return carry

    lax.fori_loop(0, 8, phase, 0)

    put_short.wait()
    def finish(side, width):
        keep(side, width).wait()
        give_back(side, width).wait_recv()
        give_back(side, width).wait_send()

    finish(1, whole)

    @pl.when(gives)
    def _():
        finish(0, part_width)
        share_q().wait_send()
        share_result(0).wait_recv()
        share_result(1).wait_recv()

    @pl.when(jnp.logical_not(gives))
    def _():
        finish(0, whole)

    @pl.when(takes)
    def _():
        share_result(0).wait_send()
        share_result(1).wait_send()

    for side in range(2):
        mate_kv(side).wait_send()
        for which in range(2):
            first_hop(side, which, 0).wait_send()
            first_hop(side, which, 1).wait_send()
            near(side, 2 + which).wait_send()
        for which in range(4):
            for piece in range(SIDE):
                far(side, piece, which).wait_send()
    mate_q().wait_send()


def on_device(long_query, long_kv, short_query, short_key_value, short_seg):
    half = long_query.shape[0]
    rows = 2 * half
    state_rows = (LOCAL_HEADS * GROUP + SHARED) * rows
    anywhere = pl.BlockSpec(memory_space=pl.ANY)
    vmem = pl.BlockSpec(memory_space=pltpu.VMEM)
    return pl.pallas_call(
        kernel,
        out_shape=(
            jax.ShapeDtypeStruct(long_query.shape, long_query.dtype),
            jax.ShapeDtypeStruct(short_query.shape, short_query.dtype),
        ),
        in_specs=[anywhere] * 4 + [vmem],
        out_specs=(anywhere, anywhere),
        scratch_shapes=[
            pltpu.VMEM((2, half, LOCAL_HEADS * WIDE), jnp.bfloat16),
            pltpu.VMEM((2, 4, 2, SIDE, rows, PAIR_WIDTH), jnp.bfloat16),
            pltpu.VMEM((state_rows, HEAD_SIZE), jnp.float32),
            pltpu.VMEM((state_rows, HEAD_SIZE), jnp.float32),
            pltpu.VMEM((state_rows, HEAD_SIZE), jnp.float32),
            pltpu.VMEM((2, 2, half, PAIR * WIDE), jnp.bfloat16),
            pltpu.VMEM((2, half, SHARED * HEAD_SIZE), jnp.bfloat16),
            pltpu.VMEM((2, half, SHARED * HEAD_SIZE), jnp.bfloat16),
            pltpu.VMEM(short_query.shape, jnp.bfloat16),
            pltpu.VMEM(short_key_value.shape, jnp.bfloat16),
            pltpu.SemaphoreType.DMA((COPIES,)),
            pltpu.SemaphoreType.DMA((COPIES,)),
            pltpu.SemaphoreType.DMA((8,)),
        ],
        compiler_params=pltpu.CompilerParams(
            collective_id=0, has_side_effects=True, vmem_limit_bytes=63 << 20
        ),
        name="window_attention",
    )(long_query, long_kv, short_query, short_key_value, short_seg)


def solution(mesh):
    return jax.shard_map(
        on_device,
        mesh=mesh,
        in_specs=(
            P(("dp", "ctx", "head"), None),
            P(None, ("dp", "ctx", "head"), None),
            P(("dp", "ctx", "head"), None),
            P(None, ("dp", "ctx", "head"), None),
            P(("dp", "ctx", "head"), None),
        ),
        out_specs=(P(("dp", "ctx", "head"), None), P(("dp", "ctx", "head"), None)),
        check_vma=False,
    )
```
